128 devices in a mesh: ctx: 32 (over z, x, core), head: 4 (over y).
Axes of the slice: x: 4, y: 4, z: 4, core: 2. Of those that a mesh axis runs over, the one named last changes fastest.
Arguments:
- queries: bfloat16 [4096, 64, 576], P('ctx', 'head'), may hold values from -104 to 104
- latent: bfloat16 [4096, 576], P('ctx'), may hold values from -6 to 6
- cotangent: bfloat16 [4096, 64, 512], P('ctx', 'head'), may hold values from -6 to 6
- selection: int32 [4096, 32], P('ctx'), may hold values from -1 to 63, as said below
Outputs:
- attended: bfloat16 [4096, 64, 512], P('ctx', 'head')
- grad_queries: bfloat16 [4096, 64, 576], P('ctx', 'head')
- grad_latent: float32 [4096, 576], P('ctx')
The draws below stay inside these ranges and needn't reach their ends.
Inputs may be any that keep to these rules, and one draw needn't show every extreme that they name: `selection`: row t lists distinct blocks, -1 in unused entries. It always lists the block of token t and never a later block. Call the 128 tokens of one index of the ctx axis a range. Besides blocks of its own range, a row lists at most one block of any other range; that range lies earlier, and all tokens of one 64-token block that list a block of a given range list the same one. So the tokens of one range list at most 2 blocks of another range. Rows of the last range always list a block of the first range. A row has unused entries only where fewer than 32 blocks are allowed by these rules.
All inputs are finite; a program needn't handle non-finite values.
Results may differ from the reference program's by a relative error of at most 0.03.
Values may be sent and summed in bfloat16 or wider, within the bound.
A program may use at most 128 MiB of HBM per device.

```python
import jax
import jax.numpy as jnp
from jax import lax

DV = 512
BLOCK = 64
TOK_DEV = 128
LATENT = 576
HEADS = 64
SEQ = 4096
SEL = 32
N_CTX = 32


def block_picks(key):
    pick_key, rank_key = jax.random.split(jax.random.fold_in(key, 23))
    shards = SEQ // TOK_DEV
    pick = jax.random.randint(pick_key, (SEQ // BLOCK, shards), 0, TOK_DEV // BLOCK)
    return (pick, rank_key)


def joint_draw(key):
    base_key = jax.random.fold_in(key, 7)
    latent_key, query_key = jax.random.split(base_key, 2)
    shards = SEQ // TOK_DEV
    latent = jax.random.truncated_normal(latent_key, -6.0, 6.0, (SEQ, LATENT), jnp.float32)
    queries = jax.random.truncated_normal(query_key, -6.0, 6.0, (SEQ, HEADS, LATENT), jnp.float32)
    pick, unused_key = block_picks(key)
    first_sums = jnp.sum(latent[:TOK_DEV].reshape(TOK_DEV // BLOCK, BLOCK, LATENT), axis=1)
    last_tokens = jnp.arange((shards - 1) * TOK_DEV, SEQ, dtype=jnp.int32)
    target = first_sums[pick[last_tokens // BLOCK, 0]]
    queries = queries.at[(shards - 1) * TOK_DEV:].add(50.0 / LATENT * target[:, None, :])
    return (queries, latent)


def draw_queries(key, part):
    queries, latent = joint_draw(key)
    return queries.astype(jnp.bfloat16)


def draw_latent(key, part):
    queries, latent = joint_draw(key)
    return latent.astype(jnp.bfloat16)


def draw_selection(key, part):
    pick, rank_key = block_picks(key)
    shards = SEQ // TOK_DEV
    blocks_here = TOK_DEV // BLOCK
    block_count = SEQ // BLOCK
    token = jnp.arange(SEQ, dtype=jnp.int32)
    query_block = token // BLOCK
    query_shard = query_block // blocks_here
    key_block = jnp.arange(block_count, dtype=jnp.int32)
    key_shard = key_block // blocks_here
    chosen = pick[query_block[:, None], key_shard[None, :]]
    remote = (key_shard[None, :] < query_shard[:, None]) & (key_block[None, :] % blocks_here == chosen)
    nearby = (key_shard[None, :] == query_shard[:, None]) & (key_block[None, :] < query_block[:, None])
    itself = key_block[None, :] == query_block[:, None]
    forced = remote & (key_shard[None, :] == 0) & (query_shard[:, None] == shards - 1)
    rank = jax.random.randint(rank_key, (SEQ, block_count), 0, 65536)
    priority = jnp.where(itself | forced, 65536, jnp.where(remote | nearby, rank, -1))
    score = priority * block_count + key_block[None, :]
    best, where_best = lax.top_k(score, SEL)
    return jnp.where(best >= 0, where_best, -1).astype(jnp.int32)


def shard_levels(rng, extent, cuts, smallest, largest):
    level, own = 1.0, jax.random.fold_in(rng, 6)
    for dim, shards_of in cuts:
        steps = jnp.exp(jax.random.uniform(jax.random.fold_in(own, dim), (shards_of,), jnp.float32, smallest / len(cuts), largest / len(cuts)))
        level = level * jnp.repeat(steps, extent[dim] // shards_of).reshape([-1 if axis == dim else 1 for axis in range(len(extent))])
    return level


def normal_values(rng, shape, width, bound, pieces=(), kind=jnp.bfloat16):
    values = jax.random.normal(rng, shape, jnp.float32) * width
    if len(pieces) > 0:
        values = shard_levels(rng, shape, pieces, -0.22, 0.18) * values
    return jnp.clip(values, min=-bound, max=bound).astype(kind)


def setup_inputs(seed: int = 0) -> dict:
    key_of = jax.random.split(jax.random.key(seed), 5)
    queries = draw_queries(jax.random.fold_in(key_of[4], 71), 0)
    latent = draw_latent(jax.random.fold_in(key_of[4], 71), 0)
    cotangent = normal_values(key_of[2], (SEQ, HEADS, DV), 1.0, 6.0, ((0, 32), (1, 4)))
    selection = draw_selection(jax.random.fold_in(key_of[4], 71), 0)
    return {"queries": queries, "latent": latent, "cotangent": cotangent, "selection": selection}


softmax_scale = 192.0 ** -0.5


def block_table(chosen, my_shard, shards, blocks_here):
    tok_rows = chosen.shape[0]
    block_count = shards * blocks_here
    picked = jnp.any(chosen[:, :, None] == jnp.arange(block_count, dtype=jnp.int32)[None, None, :], axis=1)
    grouped = picked.reshape(tok_rows, shards, blocks_here)
    own_chosen = lax.dynamic_index_in_dim(grouped, my_shard, 1, keepdims=False)
    others = jnp.arange(shards, dtype=jnp.int32) != my_shard
    per_peer = jnp.any(grouped, axis=2) & others[None, :]
    query_block = jnp.arange(tok_rows, dtype=jnp.int32) // BLOCK
    same_slot = query_block[:, None] == jnp.arange(blocks_here, dtype=jnp.int32)[None, :]
    slot_chosen = (per_peer[:, :, None] & same_slot[:, None, :]).reshape(tok_rows, shards * blocks_here)
    requested = jnp.any(grouped.reshape(blocks_here, BLOCK, shards, blocks_here), axis=1)
    wanted = jnp.sum(jnp.where(requested, jnp.arange(blocks_here, dtype=jnp.int32)[None, None, :], 0), axis=2)
    wanted = jnp.where(others[None, :], wanted, 0).T.astype(jnp.int32)
    return own_chosen, slot_chosen, wanted


def key_mask(own_chosen, slot_chosen, block_len):
    tok_rows = own_chosen.shape[0]
    position = jnp.arange(tok_rows, dtype=jnp.int32)
    own_keys = jnp.repeat(own_chosen, block_len, axis=1) & (position[None, :] <= position[:, None])
    slot_keys = jnp.repeat(slot_chosen, block_len, axis=1)
    return jnp.concatenate([own_keys, slot_keys], axis=1)


def attend(query_rows, grad_rows, key_rows, allowed):
    value_width = grad_rows.shape[1]
    latent_width = key_rows.shape[1]
    values = key_rows[:, :value_width]
    scores = jnp.dot(query_rows, key_rows.T, preferred_element_type=jnp.float32) * softmax_scale
    masked = jnp.where(allowed, scores, -jnp.inf)
    row_max = jnp.max(masked, axis=1, keepdims=True)
    row_sum = jnp.sum(jnp.exp(masked - row_max), axis=1, keepdims=True)
    log_total = row_max + jnp.log(row_sum)
    weights = jnp.exp(masked - log_total)
    weights_low = weights.astype(jnp.bfloat16)
    result = jnp.dot(weights_low, values, preferred_element_type=jnp.float32).astype(jnp.bfloat16)
    row_delta = jnp.sum(grad_rows.astype(jnp.float32) * result.astype(jnp.float32), axis=1, keepdims=True)
    grad_weights = jnp.dot(grad_rows, values.T, preferred_element_type=jnp.float32)
    grad_scores = (softmax_scale * weights * (grad_weights - row_delta)).astype(jnp.bfloat16)
    grad_query = jnp.dot(grad_scores, key_rows, preferred_element_type=jnp.float32).astype(jnp.bfloat16)
    grad_keys = jnp.dot(grad_scores.T, query_rows, preferred_element_type=jnp.float32)
    grad_values = jnp.dot(weights_low.T, grad_rows, preferred_element_type=jnp.float32)
    grad_keys = grad_keys + jnp.pad(grad_values, ((0, 0), (0, latent_width - value_width)))
    return result, grad_query, grad_keys


def reference(queries, latent, cotangent, selection):
    seq_len, heads, latent_width = queries.shape
    value_width = cotangent.shape[2]
    shards = N_CTX
    tok_rows = seq_len // shards
    blocks_here = tok_rows // BLOCK
    latent_blocks = latent.reshape(shards * blocks_here, BLOCK, latent_width)

    def shard_step(running, my_shard):
        start = (my_shard * tok_rows).astype(jnp.int32)
        query_rows = lax.dynamic_slice_in_dim(queries, start, tok_rows, 0)
        grad_rows = lax.dynamic_slice_in_dim(cotangent, start, tok_rows, 0)
        chosen = lax.dynamic_slice_in_dim(selection, start, tok_rows, 0)
        own_chosen, slot_chosen, wanted = block_table(chosen, my_shard, shards, blocks_here)
        own_latent = lax.dynamic_slice_in_dim(latent, start, tok_rows, 0)
        starts = (jnp.arange(shards, dtype=jnp.int32)[:, None] * blocks_here + wanted).reshape(-1).astype(jnp.int32)
        fetched = jnp.take(latent_blocks, starts, axis=0).reshape(shards * blocks_here * BLOCK, latent_width)
        key_rows = jnp.concatenate([own_latent, fetched], axis=0)
        allowed = jnp.repeat(key_mask(own_chosen, slot_chosen, BLOCK), heads, axis=0)
        result, grad_query, grad_keys = attend(query_rows.reshape(tok_rows * heads, latent_width), grad_rows.reshape(tok_rows * heads, value_width), key_rows, allowed)
        spread = (wanted[:, :, None] == jnp.arange(blocks_here, dtype=jnp.int32)[None, None, :]).astype(jnp.float32)
        slot_grad = grad_keys[tok_rows:].reshape(shards, blocks_here, BLOCK, latent_width)
        dense_grad = jnp.sum(spread[:, :, :, None, None] * slot_grad[:, :, None, :, :], axis=1).reshape(seq_len, latent_width)
        placed = lax.dynamic_update_slice_in_dim(jnp.zeros((seq_len, latent_width), jnp.float32), grad_keys[:tok_rows], start, 0)
        outputs = (result.reshape(tok_rows, heads, value_width), grad_query.reshape(tok_rows, heads, latent_width))
        return running + dense_grad + placed, outputs

    zeros_init = jnp.zeros((seq_len, latent_width), jnp.float32)
    grad_latent, (results, grad_queries) = lax.scan(shard_step, zeros_init, jnp.arange(shards, dtype=jnp.int32))
    attended = results.reshape(seq_len, heads, value_width)
    grad_queries = grad_queries.reshape(seq_len, heads, latent_width)
    return (attended, grad_queries, grad_latent)
```

```python
import functools

import jax
import jax.numpy as jnp
from jax import lax
from jax.experimental import pallas as pl
from jax.experimental.pallas import tpu as pltpu
from jax.sharding import PartitionSpec as P

BLOCK = 64
SCALE = 192.0 ** (-0.5)
LOG2E = 1.4426950408889634
BIG = 1e30
PLANE = 8
NT = (((1,), (1,)), ((), ()))
NN = (((1,), (0,)), ((), ()))


def dot(a, b, dims):
    return lax.dot_general(a, b, dims, preferred_element_type=jnp.float32)


def attention_kernel(
    me_ref, wanted, mask, q, do, latent, out, dq, dlat,
    qx, qt, dot_t, ksel, kx, s, p, sx, px, mrow, arow, drow, acc, accx, *, rows,
):
    shard = me_ref[0]
    plane = shard // PLANE
    width = q.shape[1]
    value = do.shape[1]
    half = BLOCK * 16
    keys = PLANE * BLOCK
    pad = qx.shape[1] - width
    c = SCALE * LOG2E

    column = lax.broadcasted_iota(jnp.int32, (BLOCK, pad), 1)

    def pick(j, carry):
        one = jnp.where(column == j, 1.0, 0.0).astype(jnp.bfloat16)
        k0 = latent[pl.ds(pl.multiple_of(j * 128, 128), 64), :]
        k1 = latent[pl.ds(pl.multiple_of(j * 128 + 64, 64), 64), :]
        at = pl.ds(pl.multiple_of(j * 64, 64), 64)
        for b in range(2):
            ksel[b, at, :width] = jnp.where(wanted[b, j] == 1, k1, k0)
            ksel[b, at, width:] = one
        return carry

    lax.fori_loop(0, (plane + 1) * PLANE, pick, 0)
    kx[:, :width] = latent[pl.ds(pl.multiple_of(shard * 128, 128), 64), :]
    kx[:, width:] = jnp.where(column == 32, 1.0, 0.0).astype(jnp.bfloat16)

    qx[:, :width] = q[...]
    qx[:, width:] = jnp.broadcast_to(mask[...][:, None, :], (128, 16, pad)).reshape(2048, pad)
    qt[...] = q[...].T

    lane = lax.broadcasted_iota(jnp.int32, (rows, keys), 1)
    row = lax.broadcasted_iota(jnp.int32, (rows, keys), 0)
    tiles = half // rows

    def row_slice(b, t):
        return pl.ds(pl.multiple_of(b * half + t * rows, rows), rows)

    def scores(g, b, own):
        at = pl.ds(pl.multiple_of(g * keys, keys), keys)

        def tile(t, carry):
            r = row_slice(b, t)
            x = dot(qx[r, :], ksel[b, at, :], NT)
            if own:
                slot = lax.rem(shard, PLANE)
                late = (lane // BLOCK == slot) & (lane % BLOCK > (row + t * rows) // 16)
                x = jnp.where(late, -BIG, x)
            s[g, r, :] = x
            top = jnp.maximum(
                jnp.maximum(x[:, 0:128], x[:, 128:256]), jnp.maximum(x[:, 256:384], x[:, 384:512])
            )
            if own:
                if b == 1:
                    y = dot(qx[r, :], kx[...], NT)
                    sx[pl.ds(pl.multiple_of(t * rows, rows), rows), :] = y
                    top = jnp.maximum(top, jnp.concatenate([y, y], axis=1))
                mrow[r, :] = top
            else:
                mrow[r, :] = jnp.maximum(mrow[r, :], top)
            return carry

        lax.fori_loop(0, tiles, tile, 0)

    scores(plane, 0, True)
    scores(plane, 1, True)

    def score_step(g, carry):
        scores(g, 0, False)
        scores(g, 1, False)
        return carry

    lax.fori_loop(0, plane, score_step, 0)

    for b in range(2):
        def tile(t, carry, b=b):
            r = row_slice(b, t)
            top = jnp.max(mrow[r, :], axis=1, keepdims=True) * c
            if b == 1:
                rx = pl.ds(pl.multiple_of(t * rows, rows), rows)
                e = jnp.exp2(sx[rx, :] * c - top)
                total = jnp.concatenate([e, jnp.zeros_like(e)], axis=1)
                e = e.astype(jnp.bfloat16)
                px[rx, :] = e
                acc = dot(e, kx[:, :value], NN)
            else:
                total = jnp.zeros((rows, 128), jnp.float32)
                acc = jnp.zeros((rows, value), jnp.float32)

            def group(g, state):
                total, acc = state
                e = jnp.exp2(s[g, r, :] * c - top)
                total = total + (e[:, 0:128] + e[:, 128:256]) + (e[:, 256:384] + e[:, 384:512])
                e = e.astype(jnp.bfloat16)
                p[g, r, :] = e
                at = pl.ds(pl.multiple_of(g * keys, keys), keys)
                acc = acc + dot(e, ksel[b, at, :value], NN)
                return total, acc

            total, acc = lax.fori_loop(0, plane + 1, group, (total, acc))
            inv = 1.0 / jnp.sum(total, axis=1, keepdims=True)
            low = (acc * inv).astype(jnp.bfloat16)
            out[r, :] = low
            delta = jnp.sum(do[r, :].astype(jnp.float32) * low.astype(jnp.float32), axis=1, keepdims=True)
            scaled = (do[r, :].astype(jnp.float32) * inv).astype(jnp.bfloat16)
            dot_t[:, r] = scaled.T
            arow[r, :] = jnp.broadcast_to(inv * SCALE, (rows, 128))
            drow[r, :] = jnp.broadcast_to(inv * SCALE * delta, (rows, 128))
            return carry

        lax.fori_loop(0, tiles, tile, 0)

    lower = lax.broadcasted_iota(jnp.int32, (width, 128), 1) < BLOCK

    def plane_grad(g, carry):
        at = pl.ds(pl.multiple_of(g * keys, keys), keys)
        for b in range(2):
            every = slice(b * half, (b + 1) * half)
            acc[b, :value, :] = dot(dot_t[:, every], p[g, every, :], NN)

            def tile(t, carry, b=b):
                r = row_slice(b, t)
                dp = dot(do[r, :], ksel[b, at, :value], NT)
                e = p[g, r, :].astype(jnp.float32)
                p[g, r, :] = (e * (dp * arow[r, 0:1] - drow[r, 0:1])).astype(jnp.bfloat16)
                return carry

            lax.fori_loop(0, tiles, tile, 0)
            dk = dot(qt[:, every], p[g, every, :], NN)
            acc[b, :value, :] += dk[:value]
            acc[b, value:, :] = dk[value:]
        for m in range(PLANE // 2):
            j = g * PLANE + 2 * m
            even = jnp.zeros((width, 128), jnp.float32)
            odd = jnp.zeros((width, 128), jnp.float32)
            for b in range(2):
                pair = acc[b, :, m * 128:(m + 1) * 128]
                rolled = pltpu.roll(pair, 64, 1)
                w0 = wanted[b, j] == 1
                w1 = wanted[b, j + 1] == 1
                even = even + jnp.where(lower ^ w0, jnp.where(w0, rolled, pair), 0.0)
                odd = odd + jnp.where(lower ^ w1, jnp.where(w1, pair, rolled), 0.0)
            dlat[j] = even.astype(dlat.dtype)
            dlat[j + 1] = odd.astype(dlat.dtype)
        return carry

    def empty(j, carry):
        dlat[j] = jnp.zeros((width, 128), dlat.dtype)
        return carry

    lax.fori_loop((plane + 1) * PLANE, dlat.shape[0], empty, 0)
    accx[:value, :] = dot(dot_t[:, half:], px[...], NN)

    def tile_x(t, carry):
        r = row_slice(1, t)
        rx = pl.ds(pl.multiple_of(t * rows, rows), rows)
        dp = dot(do[r, :], kx[:, :value], NT)
        e = px[rx, :].astype(jnp.float32)
        px[rx, :] = (e * (dp * arow[r, 0:1] - drow[r, 0:1])).astype(jnp.bfloat16)
        return carry

    lax.fori_loop(0, tiles, tile_x, 0)
    dk = dot(qt[:, half:], px[...], NN)
    accx[:value, :] += dk[:value]
    accx[value:, :] = dk[value:]

    lax.fori_loop(0, plane + 1, plane_grad, 0)
    dlat[shard, :, :BLOCK] = (dlat[shard, :, :BLOCK].astype(jnp.float32) + accx[...]).astype(dlat.dtype)

    for b in range(2):
        def tile_q(t, carry, b=b):
            r = row_slice(b, t)
            if b == 1:
                rx = pl.ds(pl.multiple_of(t * rows, rows), rows)
                total = dot(px[rx, :], kx[...], NN)
            else:
                total = jnp.zeros((rows, width + pad), jnp.float32)

            def group(g, total):
                at = pl.ds(pl.multiple_of(g * keys, keys), keys)
                return total + dot(p[g, r, :], ksel[b, at, :], NN)

            total = lax.fori_loop(0, plane + 1, group, total)
            dq[r, :] = total[:, :width].astype(jnp.bfloat16)
            return carry

        lax.fori_loop(0, tiles, tile_q, 0)


def attention(shard, wanted, mask, q, do, latent, rows=256):
    n, width = q.shape
    value = do.shape[1]
    ranges = latent.shape[0] // 128
    vmem = pl.BlockSpec(memory_space=pltpu.VMEM)
    smem = pl.BlockSpec(memory_space=pltpu.SMEM)
    planes = ranges // PLANE
    return pl.pallas_call(
        functools.partial(attention_kernel, rows=rows),
        out_shape=(
            jax.ShapeDtypeStruct((n, value), jnp.bfloat16),
            jax.ShapeDtypeStruct((n, width), jnp.bfloat16),
            jax.ShapeDtypeStruct((ranges, width, 128), jnp.bfloat16),
        ),
        in_specs=[smem, smem, vmem, vmem, vmem, vmem],
        out_specs=(vmem, vmem, vmem),
        scratch_shapes=[
            pltpu.VMEM((n, width + 64), jnp.bfloat16),
            pltpu.VMEM((width, n), jnp.bfloat16),
            pltpu.VMEM((value, n), jnp.bfloat16),
            pltpu.VMEM((2, ranges * BLOCK, width + 64), jnp.bfloat16),
            pltpu.VMEM((BLOCK, width + 64), jnp.bfloat16),
            pltpu.VMEM((planes, n, PLANE * BLOCK), jnp.float32),
            pltpu.VMEM((planes, n, PLANE * BLOCK), jnp.bfloat16),
            pltpu.VMEM((n // 2, BLOCK), jnp.float32),
            pltpu.VMEM((n // 2, BLOCK), jnp.bfloat16),
            pltpu.VMEM((n, 128), jnp.float32),
            pltpu.VMEM((n, 128), jnp.float32),
            pltpu.VMEM((n, 128), jnp.float32),
            pltpu.VMEM((2, width, PLANE * BLOCK), jnp.float32),
            pltpu.VMEM((width, BLOCK), jnp.float32),
        ],
        compiler_params=pltpu.CompilerParams(vmem_limit_bytes=67043328),
    )(shard, wanted, mask, q, do, latent)


def tables(chosen, shard, shards):
    tok = chosen.shape[0]
    picked = jnp.any(chosen[:, :, None] == jnp.arange(2 * shards, dtype=jnp.int32)[None, None, :], axis=1)
    grouped = picked.reshape(tok, shards, 2)
    mine = jnp.arange(shards, dtype=jnp.int32) == shard
    per_range = jnp.any(grouped, axis=2) | mine[None, :]
    first = jnp.any(chosen == 2 * shard, axis=1)
    allowed = jnp.concatenate([per_range, first[:, None], jnp.ones((tok, 31), bool)], axis=1)
    mask = jnp.where(allowed, 0.0, -BIG).astype(jnp.bfloat16)
    second = jnp.any(picked.reshape(2, BLOCK, shards, 2)[..., 1], axis=1)
    wanted = jnp.where(mine[None, :], jnp.arange(2)[:, None] == 1, second).astype(jnp.int32)
    return mask, wanted


def body(queries, latent, cotangent, selection):
    tok, heads, width = queries.shape
    value = cotangent.shape[2]
    shards = lax.axis_size("ctx")
    shard = lax.axis_index("ctx").astype(jnp.int32)
    mask, wanted = tables(selection, shard, shards)
    everything = lax.all_gather(latent, "ctx", axis=0, tiled=True)
    out, dq, partial = attention(
        shard[None], wanted, mask, queries.reshape(tok * heads, width),
        cotangent.reshape(tok * heads, value), everything,
    )
    own = lax.psum_scatter(partial, "ctx", scatter_dimension=0, tiled=False)
    grad = lax.psum(own.astype(jnp.float32), "head").T
    return out.reshape(tok, heads, value), dq.reshape(tok, heads, width), grad


def solution(mesh):
    placed = (P("ctx", "head", None), P("ctx", None), P("ctx", "head", None), P("ctx", None))
    return jax.shard_map(
        body,
        mesh=mesh,
        in_specs=placed,
        out_specs=(P("ctx", "head", None), P("ctx", "head", None), P("ctx", None)),
        check_vma=False,
    )
```

```python
import functools

import jax
import jax.numpy as jnp
from jax import lax
from jax.experimental import pallas as pl
from jax.experimental.pallas import tpu as pltpu
from jax.sharding import PartitionSpec as P

BLOCK = 64
SCALE = 192.0 ** (-0.5)
LOG2E = 1.4426950408889634
BIG = 1e30
PLANE = 8
NT = (((1,), (1,)), ((), ()))
NN = (((1,), (0,)), ((), ()))


def dot(a, b, dims):
    return lax.dot_general(a, b, dims, preferred_element_type=jnp.float32)


def attention_kernel(
    me_ref, wanted, mask, q, do, latent, out, dq, dlat,
    qx, qt, dot_t, ksel, kx, s, p, sx, px, mrow, arow, drow, acc, accx, *, rows,
):
    shard = me_ref[0]
    plane = shard // PLANE
    width = q.shape[1]
    value = do.shape[1]
    half = BLOCK * 16
    keys = PLANE * BLOCK
    pad = qx.shape[1] - width
    c = SCALE * LOG2E

    column = lax.broadcasted_iota(jnp.int32, (BLOCK, pad), 1)

    def pick(j, carry):
        one = jnp.where(column == j, 1.0, 0.0).astype(jnp.bfloat16)
        k0 = latent[pl.ds(pl.multiple_of(j * 128, 128), 64), :]
        k1 = latent[pl.ds(pl.multiple_of(j * 128 + 64, 64), 64), :]
        at = pl.ds(pl.multiple_of(j * 64, 64), 64)
        for b in range(2):
            ksel[b, at, :width] = jnp.where(wanted[b, j] == 1, k1, k0)
            ksel[b, at, width:] = one
        return carry

    lax.fori_loop(0, (plane + 1) * PLANE, pick, 0)
    kx[:, :width] = latent[pl.ds(pl.multiple_of(shard * 128, 128), 64), :]
    kx[:, width:] = jnp.where(column == 32, 1.0, 0.0).astype(jnp.bfloat16)

    qx[:, :width] = q[...]
    qx[:, width:] = jnp.broadcast_to(mask[...][:, None, :], (128, 16, pad)).reshape(2048, pad)
    qt[...] = q[...].T

    lane = lax.broadcasted_iota(jnp.int32, (rows, keys), 1)
    row = lax.broadcasted_iota(jnp.int32, (rows, keys), 0)
    tiles = half // rows

    def row_slice(b, t):
        return pl.ds(pl.multiple_of(b * half + t * rows, rows), rows)

    def scores(g, b, own):
        at = pl.ds(pl.multiple_of(g * keys, keys), keys)

        def tile(t, carry):
            r = row_slice(b, t)
            x = dot(qx[r, :], ksel[b, at, :], NT)
            if own:
                slot = lax.rem(shard, PLANE)
                late = (lane // BLOCK == slot) & (lane % BLOCK > (row + t * rows) // 16)
                x = jnp.where(late, -BIG, x)
            s[g, r, :] = x
            top = jnp.maximum(
                jnp.maximum(x[:, 0:128], x[:, 128:256]), jnp.maximum(x[:, 256:384], x[:, 384:512])
            )
            if own:
                if b == 1:
                    y = dot(qx[r, :], kx[...], NT)
                    sx[pl.ds(pl.multiple_of(t * rows, rows), rows), :] = y
                    top = jnp.maximum(top, jnp.concatenate([y, y], axis=1))
                mrow[r, :] = top
            else:
                mrow[r, :] = jnp.maximum(mrow[r, :], top)
            return carry

        lax.fori_loop(0, tiles, tile, 0)

    scores(plane, 0, True)
    scores(plane, 1, True)

    def score_step(g, carry):
        scores(g, 0, False)
        scores(g, 1, False)
        return carry

    lax.fori_loop(0, plane, score_step, 0)

    for b in range(2):
        def tile(t, carry, b=b):
            r = row_slice(b, t)
            top = jnp.max(mrow[r, :], axis=1, keepdims=True) * c
            if b == 1:
                rx = pl.ds(pl.multiple_of(t * rows, rows), rows)
                e = jnp.exp2(sx[rx, :] * c - top)
                total = jnp.concatenate([e, jnp.zeros_like(e)], axis=1)
                e = e.astype(jnp.bfloat16)
                px[rx, :] = e
                acc = dot(e, kx[:, :value], NN)
            else:
                total = jnp.zeros((rows, 128), jnp.float32)
                acc = jnp.zeros((rows, value), jnp.float32)

            def group(g, state):
                total, acc = state
                e = jnp.exp2(s[g, r, :] * c - top)
                total = total + (e[:, 0:128] + e[:, 128:256]) + (e[:, 256:384] + e[:, 384:512])
                e = e.astype(jnp.bfloat16)
                p[g, r, :] = e
                at = pl.ds(pl.multiple_of(g * keys, keys), keys)
                acc = acc + dot(e, ksel[b, at, :value], NN)
                return total, acc

            total, acc = lax.fori_loop(0, plane + 1, group, (total, acc))
            inv = 1.0 / jnp.sum(total, axis=1, keepdims=True)
            low = (acc * inv).astype(jnp.bfloat16)
            out[r, :] = low
            delta = jnp.sum(do[r, :].astype(jnp.float32) * low.astype(jnp.float32), axis=1, keepdims=True)
            scaled = (do[r, :].astype(jnp.float32) * inv).astype(jnp.bfloat16)
            dot_t[:, r] = scaled.T
            arow[r, :] = jnp.broadcast_to(inv * SCALE, (rows, 128))
            drow[r, :] = jnp.broadcast_to(inv * SCALE * delta, (rows, 128))
            return carry

        lax.fori_loop(0, tiles, tile, 0)

    lower = lax.broadcasted_iota(jnp.int32, (width, 128), 1) < BLOCK

    def plane_grad(g, carry):
        at = pl.ds(pl.multiple_of(g * keys, keys), keys)
        for b in range(2):
            every = slice(b * half, (b + 1) * half)
            acc[b, :value, :] = dot(dot_t[:, every], p[g, every, :], NN)

            def tile(t, carry, b=b):
                r = row_slice(b, t)
                dp = dot(do[r, :], ksel[b, at, :value], NT)
                e = p[g, r, :].astype(jnp.float32)
                p[g, r, :] = (e * (dp * arow[r, 0:1] - drow[r, 0:1])).astype(jnp.bfloat16)
                return carry

            lax.fori_loop(0, tiles, tile, 0)
            dk = dot(qt[:, every], p[g, every, :], NN)
            acc[b, :value, :] += dk[:value]
            acc[b, value:, :] = dk[value:]
        for m in range(PLANE // 2):
            j = g * PLANE + 2 * m
            even = jnp.zeros((width, 128), jnp.float32)
            odd = jnp.zeros((width, 128), jnp.float32)
            for b in range(2):
                pair = acc[b, :, m * 128:(m + 1) * 128]
                rolled = pltpu.roll(pair, 64, 1)
                w0 = wanted[b, j] == 1
                w1 = wanted[b, j + 1] == 1
                even = even + jnp.where(lower ^ w0, jnp.where(w0, rolled, pair), 0.0)
                odd = odd + jnp.where(lower ^ w1, jnp.where(w1, pair, rolled), 0.0)
            dlat[j] = even.astype(dlat.dtype)
            dlat[j + 1] = odd.astype(dlat.dtype)
        return carry

    def empty(j, carry):
        dlat[j] = jnp.zeros((width, 128), dlat.dtype)
        return carry

    lax.fori_loop((plane + 1) * PLANE, dlat.shape[0], empty, 0)
    accx[:value, :] = dot(dot_t[:, half:], px[...], NN)

    def tile_x(t, carry):
        r = row_slice(1, t)
        rx = pl.ds(pl.multiple_of(t * rows, rows), rows)
        dp = dot(do[r, :], kx[:, :value], NT)
        e = px[rx, :].astype(jnp.float32)
        px[rx, :] = (e * (dp * arow[r, 0:1] - drow[r, 0:1])).astype(jnp.bfloat16)
        return carry

    lax.fori_loop(0, tiles, tile_x, 0)
    dk = dot(qt[:, half:], px[...], NN)
    accx[:value, :] += dk[:value]
    accx[value:, :] = dk[value:]

    lax.fori_loop(0, plane + 1, plane_grad, 0)
    dlat[shard, :, :BLOCK] = (dlat[shard, :, :BLOCK].astype(jnp.float32) + accx[...]).astype(dlat.dtype)

    for b in range(2):
        def tile_q(t, carry, b=b):
            r = row_slice(b, t)
            if b == 1:
                rx = pl.ds(pl.multiple_of(t * rows, rows), rows)
                total = dot(px[rx, :], kx[...], NN)
            else:
                total = jnp.zeros((rows, width + pad), jnp.float32)

            def group(g, total):
                at = pl.ds(pl.multiple_of(g * keys, keys), keys)
                return total + dot(p[g, r, :], ksel[b, at, :], NN)

            total = lax.fori_loop(0, plane + 1, group, total)
            dq[r, :] = total[:, :width].astype(jnp.bfloat16)
            return carry

        lax.fori_loop(0, tiles, tile_q, 0)


def attention(shard, wanted, mask, q, do, latent, rows=256):
    n, width = q.shape
    value = do.shape[1]
    ranges = latent.shape[0] // 128
    vmem = pl.BlockSpec(memory_space=pltpu.VMEM)
    smem = pl.BlockSpec(memory_space=pltpu.SMEM)
    planes = ranges // PLANE
    return pl.pallas_call(
        functools.partial(attention_kernel, rows=rows),
        out_shape=(
            jax.ShapeDtypeStruct((n, value), jnp.bfloat16),
            jax.ShapeDtypeStruct((n, width), jnp.bfloat16),
            jax.ShapeDtypeStruct((ranges, width, 128), jnp.bfloat16),
        ),
        in_specs=[smem, smem, vmem, vmem, vmem, vmem],
        out_specs=(vmem, vmem, vmem),
        scratch_shapes=[
            pltpu.VMEM((n, width + 64), jnp.bfloat16),
            pltpu.VMEM((width, n), jnp.bfloat16),
            pltpu.VMEM((value, n), jnp.bfloat16),
            pltpu.VMEM((2, ranges * BLOCK, width + 64), jnp.bfloat16),
            pltpu.VMEM((BLOCK, width + 64), jnp.bfloat16),
            pltpu.VMEM((planes, n, PLANE * BLOCK), jnp.float32),
            pltpu.VMEM((planes, n, PLANE * BLOCK), jnp.bfloat16),
            pltpu.VMEM((n // 2, BLOCK), jnp.float32),
            pltpu.VMEM((n // 2, BLOCK), jnp.bfloat16),
            pltpu.VMEM((n, 128), jnp.float32),
            pltpu.VMEM((n, 128), jnp.float32),
            pltpu.VMEM((n, 128), jnp.float32),
            pltpu.VMEM((2, width, PLANE * BLOCK), jnp.float32),
            pltpu.VMEM((width, BLOCK), jnp.float32),
        ],
        compiler_params=pltpu.CompilerParams(vmem_limit_bytes=67043328),
    )(shard, wanted, mask, q, do, latent)


def tables(chosen, shard, shards):
    tok = chosen.shape[0]
    picked = jnp.any(chosen[:, :, None] == jnp.arange(2 * shards, dtype=jnp.int32)[None, None, :], axis=1)
    grouped = picked.reshape(tok, shards, 2)
    mine = jnp.arange(shards, dtype=jnp.int32) == shard
    per_range = jnp.any(grouped, axis=2) | mine[None, :]
    first = jnp.any(chosen == 2 * shard, axis=1)
    allowed = jnp.concatenate([per_range, first[:, None], jnp.ones((tok, 31), bool)], axis=1)
    mask = jnp.where(allowed, 0.0, -BIG).astype(jnp.bfloat16)
    second = jnp.any(picked.reshape(2, BLOCK, shards, 2)[..., 1], axis=1)
    wanted = jnp.where(mine[None, :], jnp.arange(2)[:, None] == 1, second).astype(jnp.int32)
    return mask, wanted


MESH_ID = pl.DeviceIdType.MESH


def ring(v, d):
    return lax.rem(v + d + 4, 4)


class Place:
    def __init__(self):
        idx = lax.axis_index("ctx").astype(jnp.int32)
        self.idx = idx
        self.z, self.x, self.c = idx // 8, lax.rem(idx // 2, 4), lax.rem(idx, 2)
        self.y = lax.axis_index("head").astype(jnp.int32)

    def at(self, dz=0, dx=0):
        return (ring(self.z, dz) * 4 + ring(self.x, dx)) * 2 + self.c

    def near(self, axis, d):
        return {"ctx": self.at(d, 0) if axis == 0 else self.at(0, d)}

    def twin(self):
        return {"ctx": self.idx + 1 - 2 * self.c}


def greet(targets):
    barrier = pltpu.get_barrier_semaphore()
    for t in targets:
        pl.semaphore_signal(barrier, inc=1, device_id=t, device_id_type=MESH_ID)
    pl.semaphore_wait(barrier, len(targets))


class Wire:
    def __init__(self, sems):
        self.sems, self.sent = sems, []

    def send(self, src, dst, recv, target):
        copy = pltpu.make_async_remote_copy(
            src_ref=src, dst_ref=dst, send_sem=self.sems.at[len(self.sent)], recv_sem=recv,
            device_id=target, device_id_type=MESH_ID,
        )
        copy.start()
        self.sent.append(copy)

    def wait(self, dst, recv, target):
        pltpu.make_async_remote_copy(
            src_ref=dst, dst_ref=dst, send_sem=self.sems.at[0], recv_sem=recv,
            device_id=target, device_id_type=MESH_ID,
        ).wait_recv()

    def finish(self):
        for copy in self.sent:
            copy.wait_send()


class Gather:
    def __init__(self, place, wire, full, recv, twin_recv):
        self.place, self.wire, self.full, self.recv, self.twin_recv = place, wire, full, recv, twin_recv

    def source(self, h, i, j):
        return self.place.at(-i, -j) if h == 0 else self.place.at(-j, -i)

    def rows(self, h, piece=None):
        return pl.ds(h * 64, 64) if piece is None else pl.ds(h * 64 + piece * 32, 32)

    def put(self, h, i, j, second, d, piece=None):
        src = self.full.at[self.source(h, i, j), self.rows(h, piece)]
        axis = (1 - h) if second else h
        ni, nj = (i, (j + d) % 4) if second else ((i + d) % 4, j)
        sem = self.recv.at[h, ni * 4 + nj, piece or 0]
        self.wire.send(src, src, sem, self.place.near(axis, d))

    def trade(self, h, i, j):
        ref = self.full.at[self.source(h, i, j), self.rows(h)]
        self.wire.send(ref, ref, self.twin_recv.at[h, i * 4 + j], self.place.twin())

    def got(self, h, i, j):
        src = self.source(h, i, j)
        pieces = (0, 1) if (j == 2 or (j == 0 and i == 2)) else (None,)
        for piece in pieces:
            self.wire.wait(self.full.at[src, self.rows(h, piece)], self.recv.at[h, i * 4 + j, piece or 0], self.place.twin())

    def both(self, h, i, j):
        self.put(h, i, j, True, 1)
        self.put(h, i, j, True, -1)

    def start(self):
        for h in range(2):
            self.put(h, 0, 0, False, 1)
            self.put(h, 0, 0, False, -1)
        for h in range(2):
            self.both(h, 0, 0)
            self.trade(h, 0, 0)

    def first(self):
        for h in range(2):
            for i, piece, d in ((1, 0, 1), (3, 1, -1)):
                self.got(h, i, 0)
                self.put(h, i, 0, False, d, piece)
                self.both(h, i, 0)
                self.trade(h, i, 0)

    def relay(self, h, i):
        for j, piece, d in ((1, 0, 1), (3, 1, -1)):
            self.got(h, i, j)
            self.put(h, i, j, True, d, piece)
            self.trade(h, i, j)

    def second(self):
        for h in range(2):
            self.relay(h, 0)
        for h in range(2):
            self.got(h, 2, 0)
            self.both(h, 2, 0)
            self.trade(h, 2, 0)

    def third(self):
        for i in (1, 3, 2):
            for h in range(2):
                self.relay(h, i)

    def last(self):
        for i in (0, 1, 3, 2):
            for h in range(2):
                self.got(h, i, 2)
                self.trade(h, i, 2)

    def traded(self):
        for i in range(4):
            for j in range(4):
                for h in range(2):
                    src = self.source(h, i, j) + 1 - 2 * self.place.c
                    self.wire.wait(self.full.at[src, self.rows(h)], self.twin_recv.at[h, i * 4 + j], self.place.twin())


def gather_kernel(own, full, sends, recv, twin_recv, local):
    place = Place()
    mine = pltpu.make_async_copy(own, full.at[place.idx], local)
    mine.start()
    greet([place.near(0, 1), place.near(0, -1), place.near(1, 1), place.near(1, -1), place.twin()])
    mine.wait()
    wire = Wire(sends)
    g = Gather(place, wire, full, recv, twin_recv)
    g.start()
    g.first()
    g.second()
    g.third()
    g.last()
    g.traded()
    wire.finish()


def gather(latent, shards):
    vmem = pl.BlockSpec(memory_space=pltpu.VMEM)
    dma = pltpu.SemaphoreType.DMA
    return pl.pallas_call(
        gather_kernel,
        out_shape=jax.ShapeDtypeStruct((shards,) + latent.shape, latent.dtype),
        in_specs=[vmem],
        out_specs=vmem,
        scratch_shapes=[dma((72,)), dma((2, 16, 2)), dma((2, 16)), dma],
        compiler_params=pltpu.CompilerParams(collective_id=0, has_side_effects=True),
    )(latent)


class Ring:
    def __init__(self, place, wire, axis, block, halves, far, near, far_sem, near_sem):
        self.place, self.wire, self.axis = place, wire, axis
        self.block, self.halves = block, halves
        self.far, self.near, self.far_sem, self.near_sem = far, near, far_sem, near_sem
        me = place.z if axis == 0 else place.x
        self.to = {d: ring(me, d) for d in (0, 1, 2, -1)}

    def start(self):
        for k, d in ((0, 1), (1, -1)):
            self.wire.send(
                self.block(self.to[2]).at[self.halves[k]], self.far.at[k], self.far_sem.at[k], self.place.near(self.axis, d)
            )

    def middle(self):
        for k, d in ((0, 1), (1, -1)):
            self.wire.wait(self.far.at[k], self.far_sem.at[k], self.place.near(self.axis, -d))
            ref = self.block(self.to[d])
            part = ref[self.halves[k]].astype(jnp.float32) + self.far[k].astype(jnp.float32)
            ref[self.halves[k]] = part.astype(ref.dtype)
            self.wire.send(ref, self.near.at[k], self.near_sem.at[k], self.place.near(self.axis, d))

    def total(self):
        for k, d in ((0, 1), (1, -1)):
            self.wire.wait(self.near.at[k], self.near_sem.at[k], self.place.near(self.axis, -d))
        mine = self.block(self.to[0])[...].astype(jnp.float32)
        return mine + (self.near[0].astype(jnp.float32) + self.near[1].astype(jnp.float32))


LOW = pl.ds(0, 288)
HIGH = pl.ds(288, 288)
PIECES = (pl.ds(0, 144), pl.ds(144, 144))


def reduce_kernel(
    part, out, twin_in, sum_a, sum_b, tot_a, tot_b, head_in, head_out, result,
    far_ax, near_ax, far_az, near_az, far_bz, near_bz, far_bx, near_bx,
    sends, twin_sem, sem_ax, sem_az, sem_bz, sem_bx, sem_y,
):
    place = Place()
    z, x, c, y = place.z, place.x, place.c, place.y
    others = [{"head": ring(y, d)} for d in (1, 2, 3)]
    greet([place.near(0, 1), place.near(0, -1), place.near(1, 1), place.near(1, -1), place.twin()] + others)
    wire = Wire(sends)
    order = [ring(z, 2), ring(z, 1), ring(z, -1), z]
    for n, g in enumerate(order):
        wire.send(part.at[g, :, 1 - c], twin_in.at[g], twin_sem.at[g], place.twin())
    b_ring = Ring(
        place, wire, 0, lambda t: sum_b.at[t], (pl.ds(0, 2), pl.ds(2, 2)), far_bz, near_bz, sem_bz.at[0], sem_bz.at[1]
    )
    a_rings = []
    for n, g in enumerate(order):
        wire.wait(twin_in.at[g], twin_sem.at[g], place.twin())
        for k in range(4):
            both = part[g, k, c].astype(jnp.float32) + twin_in[g, k].astype(jnp.float32)
            both = both.astype(part.dtype)
            sum_a[g, k] = both[:288]
            sum_b[g, k] = both[288:]
        a_ring = Ring(
            place, wire, 1, lambda t, g=g: sum_a.at[g, t], PIECES, far_ax.at[g], near_ax.at[g], sem_ax.at[g, 0], sem_ax.at[g, 1]
        )
        a_ring.start()
        if n == 0:
            b_ring.start()
        if n == 2:
            b_ring.middle()
        if n > 0:
            a_rings[n - 1].middle()
        a_rings.append(a_ring)
    a_rings[3].middle()
    tot_b[...] = b_ring.total().astype(tot_b.dtype)
    b_last = Ring(place, wire, 1, lambda t: tot_b.at[t], PIECES, far_bx, near_bx, sem_bx.at[0], sem_bx.at[1])
    b_last.start()
    a_last = Ring(place, wire, 0, lambda t: tot_a.at[t], PIECES, far_az, near_az, sem_az.at[0], sem_az.at[1])
    for n, g in enumerate(order):
        tot_a[g] = a_rings[n].total().astype(tot_a.dtype)
        if n == 0:
            a_last.start()
        if n == 2:
            a_last.middle()
    b_last.middle()
    low = a_last.total().astype(jnp.bfloat16)
    high = b_last.total().astype(jnp.bfloat16)
    for q in range(2):
        head_out[q] = low[q * 144:(q + 1) * 144]
        head_out[q + 2] = high[q * 144:(q + 1) * 144]
    for d in (1, 2, 3):
        t = ring(y, d)
        wire.send(head_out.at[t], head_in.at[d - 1], sem_y.at[0, d - 1], others[d - 1])
    for d in (1, 2, 3):
        wire.wait(head_in.at[d - 1], sem_y.at[0, d - 1], others[d - 1])
    mine = head_out[y].astype(jnp.float32) + head_in[0].astype(jnp.float32)
    mine = mine + (head_in[1].astype(jnp.float32) + head_in[2].astype(jnp.float32))
    result[y] = mine.astype(jnp.bfloat16)
    for d in (1, 2, 3):
        wire.send(result.at[y], result.at[y], sem_y.at[1, d - 1], others[d - 1])
    for d in (1, 2, 3):
        wire.wait(result.at[ring(y, -d)], sem_y.at[1, d - 1], others[d - 1])
    for q in range(4):
        out[q * 144:(q + 1) * 144, :] = result[q].astype(jnp.float32)
    wire.finish()


def reduce_all(part):
    ranges, width, lanes = part.shape
    vmem = pl.BlockSpec(memory_space=pltpu.VMEM)
    dma = pltpu.SemaphoreType.DMA
    low = jnp.bfloat16
    half, piece = width // 2, width // 4
    return pl.pallas_call(
        reduce_kernel,
        out_shape=jax.ShapeDtypeStruct((width, lanes), jnp.float32),
        in_specs=[vmem],
        out_specs=vmem,
        scratch_shapes=[
            pltpu.VMEM((4, 4, width, lanes), low),
            pltpu.VMEM((4, 4, half, lanes), low),
            pltpu.VMEM((4, 4, half, lanes), low),
            pltpu.VMEM((4, half, lanes), low),
            pltpu.VMEM((4, half, lanes), low),
            pltpu.VMEM((3, piece, lanes), low),
            pltpu.VMEM((4, piece, lanes), low),
            pltpu.VMEM((4, piece, lanes), low),
            pltpu.VMEM((4, 2, piece, lanes), low),
            pltpu.VMEM((4, 2, half, lanes), low),
            pltpu.VMEM((2, piece, lanes), low),
            pltpu.VMEM((2, half, lanes), low),
            pltpu.VMEM((2, 2, half, lanes), low),
            pltpu.VMEM((2, 4, half, lanes), low),
            pltpu.VMEM((2, piece, lanes), low),
            pltpu.VMEM((2, half, lanes), low),
            dma((40,)), dma((4,)), dma((4, 2, 2)), dma((2, 2)), dma((2, 2)), dma((2, 2)), dma((2, 3)),
        ],
        compiler_params=pltpu.CompilerParams(collective_id=1, has_side_effects=True, vmem_limit_bytes=32 << 20),
    )(part.reshape(4, 4, 2, width, lanes))


def body(queries, latent, cotangent, selection):
    tok, heads, width = queries.shape
    value = cotangent.shape[2]
    shards = lax.axis_size("ctx")
    shard = lax.axis_index("ctx").astype(jnp.int32)
    mask, wanted = tables(selection, shard, shards)
    everything = gather(latent, shards).reshape(shards * tok, width)
    out, dq, partial = attention(
        shard[None], wanted, mask, queries.reshape(tok * heads, width),
        cotangent.reshape(tok * heads, value), everything,
    )
    grad = reduce_all(partial).T
    return out.reshape(tok, heads, value), dq.reshape(tok, heads, width), grad


def solution(mesh):
    placed = (P("ctx", "head", None), P("ctx", None), P("ctx", "head", None), P("ctx", None))
    return jax.shard_map(
        body,
        mesh=mesh,
        in_specs=placed,
        out_specs=(P("ctx", "head", None), P("ctx", "head", None), P("ctx", None)),
        check_vma=False,
    )
```

```python
import functools

import jax
import jax.numpy as jnp
from jax import lax
from jax.experimental import pallas as pl
from jax.experimental.pallas import tpu as pltpu
from jax.sharding import PartitionSpec as P

BLOCK = 64
SCALE = 192.0 ** (-0.5)
LOG2E = 1.4426950408889634
BIG = 1e30
PLANE = 8
KEYS = PLANE * BLOCK
HEADS = 16
HALF = HEADS * BLOCK
NT = (((1,), (1,)), ((), ()))
NN = (((1,), (0,)), ((), ()))


def dot(a, b, dims):
    return lax.dot_general(a, b, dims, preferred_element_type=jnp.float32)


def swap(x):
    return pltpu.roll(x, 64, 1)


class Attention:
    def __init__(self, shard, wanted, width, value, refs):
        self.shard, self.wanted, self.width, self.value = shard, wanted, width, value
        (self.qx, self.qt, self.do, self.dot_t, self.ksel, self.kx, self.s, self.p, self.sx, self.px,
         self.mrow, self.arow, self.drow, self.wide, self.accx) = refs
        self.pad = self.qx.shape[1] - width

    def keys(self, g):
        return pl.ds(pl.multiple_of(g * KEYS, KEYS), KEYS)

    def block(self, b):
        return slice(b * HALF, (b + 1) * HALF)

    def load_queries(self, q, mask):
        width = self.width
        lower = lax.broadcasted_iota(jnp.int32, (width, 128), 1) < BLOCK

        def pair(m, carry):
            q0 = q[2 * m].astype(jnp.float32)
            q1 = q[2 * m + 1].astype(jnp.float32)
            for b in range(2):
                x = jnp.where(lower, q0, swap(q1)) if b == 0 else jnp.where(lower, swap(q0), q1)
                x = x.astype(jnp.bfloat16)
                at = pl.ds(pl.multiple_of(b * HALF + m * 128, 128), 128)
                self.qt[:, at] = x
                self.qx[at, :width] = x.T
                bias = mask[b * BLOCK:(b + 1) * BLOCK, :]
                self.qx[at, width:] = jnp.concatenate([bias, bias], axis=0)
            return carry

        lax.fori_loop(0, HEADS // 2, pair, 0)

    def load_cotangent(self, do):
        for b in range(2):
            for pair in range(self.value // 256):
                for k in range(2):
                    lanes = slice((2 * pair + k) * 128, (2 * pair + k + 1) * 128)
                    self.mrow[self.block(k), :] = do[self.block(b), lanes].astype(jnp.float32)

                def head(h, carry, b=b, pair=pair):
                    at = pl.ds(pl.multiple_of(b * HALF + h * BLOCK, BLOCK), BLOCK)
                    for k in range(2):
                        rows = self.mrow[pl.ds(k * HALF + h, BLOCK, stride=HEADS), :]
                        lanes = slice((2 * pair + k) * 128, (2 * pair + k + 1) * 128)
                        self.do[at, lanes] = rows.astype(jnp.bfloat16)
                    return carry

                lax.fori_loop(0, HEADS, head, 0)

    def pick(self, latent, g):
        width = self.width
        lower = lax.broadcasted_iota(jnp.int32, (width, 128), 1) < BLOCK
        column = lax.broadcasted_iota(jnp.int32, (128, self.pad), 1)
        slot = lax.broadcasted_iota(jnp.int32, (128, self.pad), 0) // BLOCK

        def pair(m, carry):
            j = g * PLANE + 2 * m
            k0 = latent[j].astype(jnp.float32)
            k1 = latent[j + 1].astype(jnp.float32)
            r0, r1 = swap(k0), swap(k1)
            at = pl.ds(pl.multiple_of(j * BLOCK, 128), 128)
            for b in range(2):
                w0, w1 = self.wanted[b, j] == 1, self.wanted[b, j + 1] == 1
                x = jnp.where(lower, jnp.where(w0, r0, k0), jnp.where(w1, k1, r1)).astype(jnp.bfloat16)
                self.ksel[b, at, :width] = x.T
                self.ksel[b, at, width:] = jnp.where(column == j + slot, 1.0, 0.0).astype(jnp.bfloat16)
            return carry

        lax.fori_loop(0, PLANE // 2, pair, 0)

    def pick_own(self, own):
        self.kx[:, :self.width] = own.T[:BLOCK, :]
        column = lax.broadcasted_iota(jnp.int32, (BLOCK, self.pad), 1)
        self.kx[:, self.width:] = jnp.where(column == 32, 1.0, 0.0).astype(jnp.bfloat16)

    def scores(self, g, b, own):
        r = self.block(b)
        x = dot(self.qx[r, :], self.ksel[b, self.keys(g), :], NT)
        if own:
            lane = lax.broadcasted_iota(jnp.int32, (HALF, KEYS), 1)
            row = lax.broadcasted_iota(jnp.int32, (HALF, KEYS), 0)
            late = (lane // BLOCK == lax.rem(self.shard, PLANE)) & (lane % BLOCK > row % BLOCK)
            x = jnp.where(late, -BIG, x)
        self.s[g] = x
        top = jnp.maximum(self.s[g, :, 0:128], self.s[g, :, 128:256])
        for k in range(2, KEYS // 128):
            top = jnp.maximum(top, self.s[g, :, k * 128:(k + 1) * 128])
        if own:
            if b == 1:
                y = dot(self.qx[r, :], self.kx[...], NT)
                self.sx[...] = y
                top = jnp.maximum(top, jnp.concatenate([y, y], axis=1))
            self.mrow[r, :] = top
        else:
            self.mrow[r, :] = jnp.maximum(self.mrow[r, :], top)

    def softmax_start(self, b):
        c = SCALE * LOG2E
        r = self.block(b)
        top = jnp.max(self.mrow[r, :], axis=1, keepdims=True) * c
        self.mrow[r, :] = jnp.broadcast_to(top, (HALF, 128))
        if b == 0:
            self.wide[r, :] = jnp.zeros((HALF, self.value), jnp.float32)
            self.arow[r, :] = jnp.zeros((HALF, 128), jnp.float32)
        else:
            e = jnp.exp2(self.sx[...] * c - top)
            self.arow[r, :] = jnp.concatenate([e, jnp.zeros_like(e)], axis=1)
            self.px[...] = e.astype(jnp.bfloat16)
            self.wide[r, :] = dot(self.px[...], self.kx[:, :self.value], NN)

    def softmax(self, g, b):
        c = SCALE * LOG2E
        r = self.block(b)
        total = self.arow[r, :]
        for k in range(KEYS // 128):
            lanes = slice(k * 128, (k + 1) * 128)
            e = jnp.exp2(self.s[g, :, lanes] * c - self.mrow[r, :])
            total = total + e
            self.p[g, r, lanes] = e.astype(jnp.bfloat16)
        self.arow[r, :] = total
        self.wide[r, :] += dot(self.p[g, r, :], self.ksel[b, self.keys(g), :self.value], NN)

    def softmax_end(self, b, out):
        def tile(t, carry):
            r = pl.ds(pl.multiple_of(b * HALF + t * 256, 256), 256)
            inv = 1.0 / jnp.sum(self.arow[r, :], axis=1, keepdims=True)
            full = self.wide[r, :] * inv
            self.wide[r, :] = full
            do = self.do[r, :].astype(jnp.float32)
            delta = jnp.sum(do * full.astype(jnp.bfloat16).astype(jnp.float32), axis=1, keepdims=True)
            self.dot_t[:, r] = (do * inv).astype(jnp.bfloat16).T
            self.arow[r, :] = jnp.broadcast_to(inv * SCALE, (256, 128))
            self.drow[r, :] = jnp.broadcast_to(inv * SCALE * delta, (256, 128))
            return carry

        lax.fori_loop(0, HALF // 256, tile, 0)
        for k in range(self.value // 128):
            lanes = slice(k * 128, (k + 1) * 128)
            self.mrow[self.block(b), :] = self.wide[self.block(b), lanes]

            def token(t, carry, lanes=lanes):
                at = pl.ds(pl.multiple_of((b * BLOCK + t) * HEADS, HEADS), HEADS)
                out[at, lanes] = self.mrow[pl.ds(b * HALF + t, HEADS, stride=BLOCK), :].astype(jnp.bfloat16)
                return carry

            lax.fori_loop(0, BLOCK, token, 0, unroll=8)

    def acc(self, b, at):
        return self.s.at[2 + b, at]

    def grads(self, g):
        value, width = self.value, self.width
        for b in range(2):
            r = self.block(b)
            top, rest = self.acc(b, slice(0, value)), self.acc(b, slice(value, width))
            top[...] = dot(self.dot_t[:, r], self.p[g, r, :], NN)
            self.s[b] = dot(self.do[r, :], self.ksel[b, self.keys(g), :value], NT)
            for k in range(KEYS // 128):
                lanes = slice(k * 128, (k + 1) * 128)
                e = self.p[g, r, lanes].astype(jnp.float32)
                d = e * (self.s[b, :, lanes] * self.arow[r, :] - self.drow[r, :])
                self.p[g, r, lanes] = d.astype(jnp.bfloat16)
            dk = dot(self.qt[:, r], self.p[g, r, :], NN)
            top[...] += dk[:value]
            rest[...] = dk[value:]

    def grads_extra(self):
        value, r = self.value, self.block(1)
        self.accx[:value, :] = dot(self.dot_t[:, r], self.px[...], NN)
        dp = dot(self.do[r, :], self.kx[:, :value], NT)
        e = self.px[...].astype(jnp.float32)
        self.px[...] = (e * (dp * self.arow[r, 0:BLOCK] - self.drow[r, 0:BLOCK])).astype(jnp.bfloat16)
        dk = dot(self.qt[:, r], self.px[...], NN)
        self.accx[:value, :] += dk[:value]
        self.accx[value:, :] = dk[value:]

    def spread(self, g, m):
        lower = lax.broadcasted_iota(jnp.int32, (self.width, 128), 1) < BLOCK
        j = g * PLANE + 2 * m
        even = jnp.zeros((self.width, 128), jnp.float32)
        odd = jnp.zeros((self.width, 128), jnp.float32)
        for b in range(2):
            x = self.acc(b, slice(0, self.width))[:, m * 128:(m + 1) * 128]
            rolled = swap(x)
            w0 = self.wanted[b, j] == 1
            w1 = self.wanted[b, j + 1] == 1
            even = even + jnp.where(lower ^ w0, jnp.where(w0, rolled, x), 0.0)
            odd = odd + jnp.where(lower ^ w1, jnp.where(w1, x, rolled), 0.0)
        return even, odd

    def wide_at(self, b, n):
        at = (2 * b + n) * self.width
        return pl.ds(at, self.width)

    def grad_queries_start(self):
        for n in range(2):
            self.wide[self.wide_at(0, n), :] = jnp.zeros((self.width, HALF // 2), jnp.float32)
            rows = self.px[n * HALF // 2:(n + 1) * HALF // 2, :]
            self.wide[self.wide_at(1, n), :] = dot(self.kx[:, :self.width].T, rows, NT)

    def grad_queries(self, g):
        for b in range(2):
            kt = self.ksel[b, self.keys(g), :self.width].T
            for n in range(2):
                rows = self.p[g, b * HALF + n * HALF // 2:b * HALF + (n + 1) * HALF // 2, :]
                self.wide[self.wide_at(b, n), :] += dot(kt, rows, NT)

    def grad_queries_end(self, dq):
        lower = lax.broadcasted_iota(jnp.int32, (self.width, 128), 1) < BLOCK
        for m in range(HEADS // 2):
            n, lanes = m // 4, slice((m % 4) * 128, (m % 4 + 1) * 128)
            y0 = self.wide[self.wide_at(0, n), lanes]
            y1 = self.wide[self.wide_at(1, n), lanes]
            dq[2 * m] = jnp.where(lower, y0, swap(y1)).astype(jnp.bfloat16)
            dq[2 * m + 1] = jnp.where(lower, swap(y0), y1).astype(jnp.bfloat16)


def scratch(width, value, ranges):
    n, low, f32 = 2 * HALF, jnp.bfloat16, jnp.float32
    planes = ranges // PLANE
    return [
        pltpu.VMEM((n, width + 64), low),
        pltpu.VMEM((width, n), low),
        pltpu.VMEM((n, value), low),
        pltpu.VMEM((value, n), low),
        pltpu.VMEM((2, ranges * BLOCK, width + 64), low),
        pltpu.VMEM((BLOCK, width + 64), low),
        pltpu.VMEM((planes, HALF, KEYS), f32),
        pltpu.VMEM((planes, n, KEYS), low),
        pltpu.VMEM((HALF, BLOCK), f32),
        pltpu.VMEM((HALF, BLOCK), low),
        pltpu.VMEM((n, 128), f32),
        pltpu.VMEM((n, 128), f32),
        pltpu.VMEM((n, 128), f32),
        pltpu.VMEM((4 * width, HALF // 2), f32),
        pltpu.VMEM((width, BLOCK), f32),
    ]


def attention_kernel(me_ref, wanted, mask, q_in, do_in, latent, out_hbm, dq_hbm, dlat, q, do, sems, *refs):
    shard = me_ref[0]
    plane = shard // PLANE
    width = q.shape[1]
    out, dq = do, q
    a = Attention(shard, wanted, width, do.shape[1], refs)
    get_q = pltpu.make_async_copy(q_in, q, sems.at[0])
    get_do = pltpu.make_async_copy(do_in, do, sems.at[1])
    put_out = pltpu.make_async_copy(out, out_hbm, sems.at[2])
    put_dq = pltpu.make_async_copy(dq, dq_hbm, sems.at[3])
    get_q.start()
    get_do.start()
    get_q.wait()
    get_do.wait()

    def each(count, step):
        def body(g, carry):
            step(g)
            return carry

        lax.fori_loop(0, count, body, 0)

    a.load_queries(q, mask)
    a.load_cotangent(do)
    each(plane + 1, lambda g: a.pick(latent, g))
    a.pick_own(latent[shard])
    for b in range(2):
        a.scores(plane, b, True)
        each(plane, lambda g, b=b: a.scores(g, b, False))
        a.softmax_start(b)
        each(plane + 1, lambda g, b=b: a.softmax(g, b))
        a.softmax_end(b, out)
    put_out.start()
    a.grads_extra()

    def grads(g):
        a.grads(g)
        for m in range(PLANE // 2):
            even, odd = a.spread(g, m)
            j = g * PLANE + 2 * m
            dlat[j] = even.astype(dlat.dtype)
            dlat[j + 1] = odd.astype(dlat.dtype)

    def empty(j, carry):
        dlat[j] = jnp.zeros(dlat.shape[1:], dlat.dtype)
        return carry

    each(plane + 1, grads)
    lax.fori_loop((plane + 1) * PLANE, dlat.shape[0], empty, 0)
    dlat[shard, :, :BLOCK] = (dlat[shard, :, :BLOCK].astype(jnp.float32) + a.accx[...]).astype(dlat.dtype)
    a.grad_queries_start()
    each(plane + 1, a.grad_queries)
    a.grad_queries_end(dq)
    put_dq.start()
    put_dq.wait()
    put_out.wait()


def attention(shard, wanted, mask, q, do, latent):
    heads, width, tok = q.shape
    value = do.shape[1]
    ranges = latent.shape[0]
    vmem = pl.BlockSpec(memory_space=pltpu.VMEM)
    smem = pl.BlockSpec(memory_space=pltpu.SMEM)
    hbm = pl.BlockSpec(memory_space=pl.ANY)
    return pl.pallas_call(
        attention_kernel,
        out_shape=(
            jax.ShapeDtypeStruct((heads * tok, value), jnp.bfloat16),
            jax.ShapeDtypeStruct((heads, width, tok), jnp.bfloat16),
            jax.ShapeDtypeStruct((ranges, width, tok), jnp.bfloat16),
        ),
        in_specs=[smem, smem, vmem, hbm, hbm, vmem],
        out_specs=(hbm, hbm, vmem),
        scratch_shapes=[
            pltpu.VMEM(q.shape, q.dtype), pltpu.VMEM(do.shape, do.dtype), pltpu.SemaphoreType.DMA((4,)),
        ] + scratch(width, value, ranges),
        compiler_params=pltpu.CompilerParams(vmem_limit_bytes=67043328),
    )(shard, wanted, mask, q, do, latent)


def tables(chosen, shard, shards):
    tok = chosen.shape[0]
    picked = jnp.any(chosen[:, :, None] == jnp.arange(2 * shards, dtype=jnp.int32)[None, None, :], axis=1)
    grouped = picked.reshape(tok, shards, 2)
    mine = jnp.arange(shards, dtype=jnp.int32) == shard
    per_range = jnp.any(grouped, axis=2) | mine[None, :]
    first = jnp.any(chosen == 2 * shard, axis=1)
    allowed = jnp.concatenate([per_range, first[:, None], jnp.ones((tok, 31), bool)], axis=1)
    mask = jnp.where(allowed, 0.0, -BIG).astype(jnp.bfloat16)
    second = jnp.any(picked.reshape(2, BLOCK, shards, 2)[..., 1], axis=1)
    wanted = jnp.where(mine[None, :], jnp.arange(2)[:, None] == 1, second).astype(jnp.int32)
    return mask, wanted


MESH_ID = pl.DeviceIdType.MESH


def ring(v, d):
    return lax.rem(v + d + 4, 4)


class Place:
    def __init__(self):
        idx = lax.axis_index("ctx").astype(jnp.int32)
        self.idx = idx
        self.z, self.x, self.c = idx // 8, lax.rem(idx // 2, 4), lax.rem(idx, 2)
        self.y = lax.axis_index("head").astype(jnp.int32)

    def at(self, dz=0, dx=0):
        return (ring(self.z, dz) * 4 + ring(self.x, dx)) * 2 + self.c

    def near(self, axis, d):
        return {"ctx": self.at(d, 0) if axis == 0 else self.at(0, d)}

    def twin(self):
        return {"ctx": self.idx + 1 - 2 * self.c}


def greet(targets):
    barrier = pltpu.get_barrier_semaphore()
    for t in targets:
        pl.semaphore_signal(barrier, inc=1, device_id=t, device_id_type=MESH_ID)
    pl.semaphore_wait(barrier, len(targets))


class Wire:
    def __init__(self, sems):
        self.sems, self.sent = sems, []

    def send(self, src, dst, recv, target):
        copy = pltpu.make_async_remote_copy(
            src_ref=src, dst_ref=dst, send_sem=self.sems.at[len(self.sent)], recv_sem=recv,
            device_id=target, device_id_type=MESH_ID,
        )
        copy.start()
        self.sent.append(copy)

    def wait(self, dst, recv, target):
        pltpu.make_async_remote_copy(
            src_ref=dst, dst_ref=dst, send_sem=self.sems.at[0], recv_sem=recv,
            device_id=target, device_id_type=MESH_ID,
        ).wait_recv()

    def finish(self):
        for copy in self.sent:
            copy.wait_send()


class Gather:
    def __init__(self, place, wire, full, recv, twin_recv):
        self.place, self.wire, self.full, self.recv, self.twin_recv = place, wire, full, recv, twin_recv

    def source(self, h, i, j):
        return self.place.at(-i, -j) if h == 0 else self.place.at(-j, -i)

    def rows(self, h, piece=None):
        return pl.ds(h * 288, 288) if piece is None else pl.ds(h * 288 + piece * 144, 144)

    def put(self, h, i, j, second, d, piece=None):
        src = self.full.at[self.source(h, i, j), self.rows(h, piece)]
        axis = (1 - h) if second else h
        ni, nj = (i, (j + d) % 4) if second else ((i + d) % 4, j)
        sem = self.recv.at[h, ni * 4 + nj, piece or 0]
        self.wire.send(src, src, sem, self.place.near(axis, d))

    def trade(self, h, i, j):
        ref = self.full.at[self.source(h, i, j), self.rows(h)]
        self.wire.send(ref, ref, self.twin_recv.at[h, i * 4 + j], self.place.twin())

    def got(self, h, i, j):
        src = self.source(h, i, j)
        pieces = (0, 1) if (j == 2 or (j == 0 and i == 2)) else (None,)
        for piece in pieces:
            self.wire.wait(self.full.at[src, self.rows(h, piece)], self.recv.at[h, i * 4 + j, piece or 0], self.place.twin())

    def both(self, h, i, j):
        self.put(h, i, j, True, 1)
        self.put(h, i, j, True, -1)

    def start(self):
        for h in range(2):
            self.put(h, 0, 0, False, 1)
            self.put(h, 0, 0, False, -1)
        for h in range(2):
            self.both(h, 0, 0)
            self.trade(h, 0, 0)

    def first(self):
        for h in range(2):
            for i, piece, d in ((1, 0, 1), (3, 1, -1)):
                self.got(h, i, 0)
                self.put(h, i, 0, False, d, piece)
                self.both(h, i, 0)
                self.trade(h, i, 0)

    def relay(self, h, i):
        for j, piece, d in ((1, 0, 1), (3, 1, -1)):
            self.got(h, i, j)
            self.put(h, i, j, True, d, piece)
            self.trade(h, i, j)

    def second(self):
        for h in range(2):
            self.relay(h, 0)
        for h in range(2):
            self.got(h, 2, 0)
            self.both(h, 2, 0)
            self.trade(h, 2, 0)

    def third(self):
        for i in (1, 3, 2):
            for h in range(2):
                self.relay(h, i)

    def last(self):
        for i in (0, 1, 3, 2):
            for h in range(2):
                self.got(h, i, 2)
                self.trade(h, i, 2)

    def traded(self):
        for i in range(4):
            for j in range(4):
                for h in range(2):
                    src = self.source(h, i, j) + 1 - 2 * self.place.c
                    self.wire.wait(self.full.at[src, self.rows(h)], self.twin_recv.at[h, i * 4 + j], self.place.twin())


def gather_kernel(own, full, sends, recv, twin_recv, local):
    place = Place()
    mine = pltpu.make_async_copy(own, full.at[place.idx], local)
    mine.start()
    greet([place.near(0, 1), place.near(0, -1), place.near(1, 1), place.near(1, -1), place.twin()])
    mine.wait()
    wire = Wire(sends)
    g = Gather(place, wire, full, recv, twin_recv)
    g.start()
    g.first()
    g.second()
    g.third()
    g.last()
    g.traded()
    wire.finish()


def gather(latent, shards):
    vmem = pl.BlockSpec(memory_space=pltpu.VMEM)
    dma = pltpu.SemaphoreType.DMA
    return pl.pallas_call(
        gather_kernel,
        out_shape=jax.ShapeDtypeStruct((shards,) + latent.shape, latent.dtype),
        in_specs=[vmem],
        out_specs=vmem,
        scratch_shapes=[dma((72,)), dma((2, 16, 2)), dma((2, 16)), dma],
        compiler_params=pltpu.CompilerParams(collective_id=0, has_side_effects=True),
    )(latent)


class Ring:
    def __init__(self, place, wire, axis, block, halves, far, near, far_sem, near_sem):
        self.place, self.wire, self.axis = place, wire, axis
        self.block, self.halves = block, halves
        self.far, self.near, self.far_sem, self.near_sem = far, near, far_sem, near_sem
        me = place.z if axis == 0 else place.x
        self.to = {d: ring(me, d) for d in (0, 1, 2, -1)}

    def start(self):
        for k, d in ((0, 1), (1, -1)):
            self.wire.send(
                self.block(self.to[2]).at[self.halves[k]], self.far.at[k], self.far_sem.at[k], self.place.near(self.axis, d)
            )

    def middle(self):
        for k, d in ((0, 1), (1, -1)):
            self.wire.wait(self.far.at[k], self.far_sem.at[k], self.place.near(self.axis, -d))
            ref = self.block(self.to[d])
            part = ref[self.halves[k]].astype(jnp.float32) + self.far[k].astype(jnp.float32)
            ref[self.halves[k]] = part.astype(ref.dtype)
            self.wire.send(ref, self.near.at[k], self.near_sem.at[k], self.place.near(self.axis, d))

    def total(self):
        for k, d in ((0, 1), (1, -1)):
            self.wire.wait(self.near.at[k], self.near_sem.at[k], self.place.near(self.axis, -d))
        mine = self.block(self.to[0])[...].astype(jnp.float32)
        return mine + (self.near[0].astype(jnp.float32) + self.near[1].astype(jnp.float32))


LOW = pl.ds(0, 288)
HIGH = pl.ds(288, 288)
PIECES = (pl.ds(0, 144), pl.ds(144, 144))


def reduce_kernel(
    part, out, twin_in, sum_a, sum_b, tot_a, tot_b, head_in, head_out, result,
    far_ax, near_ax, far_az, near_az, far_bz, near_bz, far_bx, near_bx,
    sends, twin_sem, sem_ax, sem_az, sem_bz, sem_bx, sem_y,
):
    place = Place()
    z, x, c, y = place.z, place.x, place.c, place.y
    others = [{"head": ring(y, d)} for d in (1, 2, 3)]
    greet([place.near(0, 1), place.near(0, -1), place.near(1, 1), place.near(1, -1), place.twin()] + others)
    wire = Wire(sends)
    order = [ring(z, 2), ring(z, 1), ring(z, -1), z]
    for n, g in enumerate(order):
        wire.send(part.at[g, :, 1 - c], twin_in.at[g], twin_sem.at[g], place.twin())
    b_ring = Ring(
        place, wire, 0, lambda t: sum_b.at[t], (pl.ds(0, 2), pl.ds(2, 2)), far_bz, near_bz, sem_bz.at[0], sem_bz.at[1]
    )
    a_rings = []
    for n, g in enumerate(order):
        wire.wait(twin_in.at[g], twin_sem.at[g], place.twin())
        for k in range(4):
            both = part[g, k, c].astype(jnp.float32) + twin_in[g, k].astype(jnp.float32)
            both = both.astype(part.dtype)
            sum_a[g, k] = both[:288]
            sum_b[g, k] = both[288:]
        a_ring = Ring(
            place, wire, 1, lambda t, g=g: sum_a.at[g, t], PIECES, far_ax.at[g], near_ax.at[g], sem_ax.at[g, 0], sem_ax.at[g, 1]
        )
        a_ring.start()
        if n == 0:
            b_ring.start()
        if n == 2:
            b_ring.middle()
        if n > 0:
            a_rings[n - 1].middle()
        a_rings.append(a_ring)
    a_rings[3].middle()
    tot_b[...] = b_ring.total().astype(tot_b.dtype)
    b_last = Ring(place, wire, 1, lambda t: tot_b.at[t], PIECES, far_bx, near_bx, sem_bx.at[0], sem_bx.at[1])
    b_last.start()
    a_last = Ring(place, wire, 0, lambda t: tot_a.at[t], PIECES, far_az, near_az, sem_az.at[0], sem_az.at[1])
    for n, g in enumerate(order):
        tot_a[g] = a_rings[n].total().astype(tot_a.dtype)
        if n == 0:
            a_last.start()
        if n == 2:
            a_last.middle()
    b_last.middle()
    low = a_last.total().astype(jnp.bfloat16)
    high = b_last.total().astype(jnp.bfloat16)
    for q in range(2):
        head_out[q] = low[q * 144:(q + 1) * 144]
        head_out[q + 2] = high[q * 144:(q + 1) * 144]
    for d in (1, 2, 3):
        t = ring(y, d)
        wire.send(head_out.at[t], head_in.at[d - 1], sem_y.at[0, d - 1], others[d - 1])
    for d in (1, 2, 3):
        wire.wait(head_in.at[d - 1], sem_y.at[0, d - 1], others[d - 1])
    mine = head_out[y].astype(jnp.float32) + head_in[0].astype(jnp.float32)
    mine = mine + (head_in[1].astype(jnp.float32) + head_in[2].astype(jnp.float32))
    result[y] = mine.astype(jnp.bfloat16)
    for d in (1, 2, 3):
        wire.send(result.at[y], result.at[y], sem_y.at[1, d - 1], others[d - 1])
    for d in (1, 2, 3):
        wire.wait(result.at[ring(y, -d)], sem_y.at[1, d - 1], others[d - 1])
    for q in range(4):
        out[q * 144:(q + 1) * 144, :] = result[q].astype(jnp.float32)
    wire.finish()


def reduce_all(part):
    ranges, width, lanes = part.shape
    vmem = pl.BlockSpec(memory_space=pltpu.VMEM)
    dma = pltpu.SemaphoreType.DMA
    low = jnp.bfloat16
    half, piece = width // 2, width // 4
    return pl.pallas_call(
        reduce_kernel,
        out_shape=jax.ShapeDtypeStruct((width, lanes), jnp.float32),
        in_specs=[vmem],
        out_specs=vmem,
        scratch_shapes=[
            pltpu.VMEM((4, 4, width, lanes), low),
            pltpu.VMEM((4, 4, half, lanes), low),
            pltpu.VMEM((4, 4, half, lanes), low),
            pltpu.VMEM((4, half, lanes), low),
            pltpu.VMEM((4, half, lanes), low),
            pltpu.VMEM((3, piece, lanes), low),
            pltpu.VMEM((4, piece, lanes), low),
            pltpu.VMEM((4, piece, lanes), low),
            pltpu.VMEM((4, 2, piece, lanes), low),
            pltpu.VMEM((4, 2, half, lanes), low),
            pltpu.VMEM((2, piece, lanes), low),
            pltpu.VMEM((2, half, lanes), low),
            pltpu.VMEM((2, 2, half, lanes), low),
            pltpu.VMEM((2, 4, half, lanes), low),
            pltpu.VMEM((2, piece, lanes), low),
            pltpu.VMEM((2, half, lanes), low),
            dma((40,)), dma((4,)), dma((4, 2, 2)), dma((2, 2)), dma((2, 2)), dma((2, 2)), dma((2, 3)),
        ],
        compiler_params=pltpu.CompilerParams(collective_id=1, has_side_effects=True, vmem_limit_bytes=32 << 20),
    )(part.reshape(4, 4, 2, width, lanes))


def body(queries, latent, cotangent, selection):
    tok, heads, width = queries.shape
    value = cotangent.shape[2]
    shards = lax.axis_size("ctx")
    shard = lax.axis_index("ctx").astype(jnp.int32)
    mask, wanted = tables(selection, shard, shards)
    everything = gather(latent.T, shards)
    out, dq, partial = attention(
        shard[None], wanted, mask, queries.transpose(1, 2, 0), cotangent.reshape(tok * heads, value), everything
    )
    grad = reduce_all(partial).T
    return out.reshape(tok, heads, value), dq.transpose(2, 0, 1), grad


def solution(mesh):
    placed = (P("ctx", "head", None), P("ctx", None), P("ctx", "head", None), P("ctx", None))
    return jax.shard_map(
        body,
        mesh=mesh,
        in_specs=placed,
        out_specs=(P("ctx", "head", None), P("ctx", "head", None), P("ctx", None)),
        check_vma=False,
    )
```

```python
import functools

import jax
import jax.numpy as jnp
from jax import lax
from jax.experimental import pallas as pl
from jax.experimental.pallas import tpu as pltpu
from jax.sharding import PartitionSpec as P

BLOCK = 64
SCALE = 192.0 ** (-0.5)
LOG2E = 1.4426950408889634
BIG = 1e30
PLANE = 8
KEYS = PLANE * BLOCK
HEADS = 16
HALF = HEADS * BLOCK
NT = (((1,), (1,)), ((), ()))
NN = (((1,), (0,)), ((), ()))


def dot(a, b, dims):
    return lax.dot_general(a, b, dims, preferred_element_type=jnp.float32)


def swap(x):
    return pltpu.roll(x, 64, 1)


class Attention:
    def __init__(self, shard, wanted, width, value, refs):
        self.shard, self.wanted, self.width, self.value = shard, wanted, width, value
        (self.qx, self.qt, self.do, self.dot_t, self.ksel, self.kx, self.s, self.p, self.sx, self.px,
         self.mrow, self.arow, self.drow, self.wide, self.accx) = refs
        self.pad = self.qx.shape[1] - width

    def keys(self, g):
        return pl.ds(pl.multiple_of(g * KEYS, KEYS), KEYS)

    def block(self, b):
        return slice(b * HALF, (b + 1) * HALF)

    def load_queries(self, q, mask):
        width = self.width
        lower = lax.broadcasted_iota(jnp.int32, (width, 128), 1) < BLOCK

        def pair(m, carry):
            q0 = q[2 * m].astype(jnp.float32)
            q1 = q[2 * m + 1].astype(jnp.float32)
            for b in range(2):
                x = jnp.where(lower, q0, swap(q1)) if b == 0 else jnp.where(lower, swap(q0), q1)
                x = x.astype(jnp.bfloat16)
                at = pl.ds(pl.multiple_of(b * HALF + m * 128, 128), 128)
                self.qt[:, at] = x
                self.qx[at, :width] = x.T
                bias = mask[b * BLOCK:(b + 1) * BLOCK, :]
                self.qx[at, width:] = jnp.concatenate([bias, bias], axis=0)
            return carry

        lax.fori_loop(0, HEADS // 2, pair, 0)

    def load_cotangent(self, do):
        for b in range(2):
            for pair in range(self.value // 256):
                for k in range(2):
                    lanes = slice((2 * pair + k) * 128, (2 * pair + k + 1) * 128)
                    self.mrow[self.block(k), :] = do[self.block(b), lanes].astype(jnp.float32)

                def head(h, carry, b=b, pair=pair):
                    at = pl.ds(pl.multiple_of(b * HALF + h * BLOCK, BLOCK), BLOCK)
                    for k in range(2):
                        rows = self.mrow[pl.ds(k * HALF + h, BLOCK, stride=HEADS), :]
                        lanes = slice((2 * pair + k) * 128, (2 * pair + k + 1) * 128)
                        self.do[at, lanes] = rows.astype(jnp.bfloat16)
                    return carry

                lax.fori_loop(0, HEADS, head, 0)

    def pick(self, latent, g):
        width = self.width
        lower = lax.broadcasted_iota(jnp.int32, (width, 128), 1) < BLOCK
        column = lax.broadcasted_iota(jnp.int32, (128, self.pad), 1)
        slot = lax.broadcasted_iota(jnp.int32, (128, self.pad), 0) // BLOCK

        def pair(m, carry):
            j = g * PLANE + 2 * m
            k0 = latent[j].astype(jnp.float32)
            k1 = latent[j + 1].astype(jnp.float32)
            r0, r1 = swap(k0), swap(k1)
            at = pl.ds(pl.multiple_of(j * BLOCK, 128), 128)
            for b in range(2):
                w0, w1 = self.wanted[b, j] == 1, self.wanted[b, j + 1] == 1
                x = jnp.where(lower, jnp.where(w0, r0, k0), jnp.where(w1, k1, r1)).astype(jnp.bfloat16)
                self.ksel[b, at, :width] = x.T
                self.ksel[b, at, width:] = jnp.where(column == j + slot, 1.0, 0.0).astype(jnp.bfloat16)
            return carry

        lax.fori_loop(0, PLANE // 2, pair, 0)

    def pick_own(self, own):
        self.kx[:, :self.width] = own.T[:BLOCK, :]
        column = lax.broadcasted_iota(jnp.int32, (BLOCK, self.pad), 1)
        self.kx[:, self.width:] = jnp.where(column == 32, 1.0, 0.0).astype(jnp.bfloat16)

    def scores(self, g, b, own):
        r = self.block(b)
        x = dot(self.qx[r, :], self.ksel[b, self.keys(g), :], NT)
        if own:
            lane = lax.broadcasted_iota(jnp.int32, (HALF, KEYS), 1)
            row = lax.broadcasted_iota(jnp.int32, (HALF, KEYS), 0)
            late = (lane // BLOCK == lax.rem(self.shard, PLANE)) & (lane % BLOCK > row % BLOCK)
            x = jnp.where(late, -BIG, x)
        self.s[g] = x
        top = jnp.maximum(self.s[g, :, 0:128], self.s[g, :, 128:256])
        for k in range(2, KEYS // 128):
            top = jnp.maximum(top, self.s[g, :, k * 128:(k + 1) * 128])
        if own:
            if b == 1:
                y = dot(self.qx[r, :], self.kx[...], NT)
                self.sx[...] = y
                top = jnp.maximum(top, jnp.concatenate([y, y], axis=1))
            self.mrow[r, :] = top
        else:
            self.mrow[r, :] = jnp.maximum(self.mrow[r, :], top)

    def softmax_start(self, b):
        c = SCALE * LOG2E
        r = self.block(b)
        top = jnp.max(self.mrow[r, :], axis=1, keepdims=True) * c
        self.mrow[r, :] = jnp.broadcast_to(top, (HALF, 128))
        if b == 0:
            self.wide[r, :] = jnp.zeros((HALF, self.value), jnp.float32)
            self.arow[r, :] = jnp.zeros((HALF, 128), jnp.float32)
        else:
            e = jnp.exp2(self.sx[...] * c - top)
            self.arow[r, :] = jnp.concatenate([e, jnp.zeros_like(e)], axis=1)
            self.px[...] = e.astype(jnp.bfloat16)
            self.wide[r, :] = dot(self.px[...], self.kx[:, :self.value], NN)

    def softmax(self, g, b):
        c = SCALE * LOG2E
        r = self.block(b)
        total = self.arow[r, :]
        for k in range(KEYS // 128):
            lanes = slice(k * 128, (k + 1) * 128)
            e = jnp.exp2(self.s[g, :, lanes] * c - self.mrow[r, :])
            total = total + e
            self.p[g, r, lanes] = e.astype(jnp.bfloat16)
        self.arow[r, :] = total
        self.wide[r, :] += dot(self.p[g, r, :], self.ksel[b, self.keys(g), :self.value], NN)

    def softmax_end(self, b, out):
        def tile(t, carry):
            r = pl.ds(pl.multiple_of(b * HALF + t * 256, 256), 256)
            inv = 1.0 / jnp.sum(self.arow[r, :], axis=1, keepdims=True)
            full = self.wide[r, :] * inv
            self.wide[r, :] = full
            do = self.do[r, :].astype(jnp.float32)
            delta = jnp.sum(do * full.astype(jnp.bfloat16).astype(jnp.float32), axis=1, keepdims=True)
            self.dot_t[:, r] = (do * inv).astype(jnp.bfloat16).T
            self.arow[r, :] = jnp.broadcast_to(inv * SCALE, (256, 128))
            self.drow[r, :] = jnp.broadcast_to(inv * SCALE * delta, (256, 128))
            return carry

        lax.fori_loop(0, HALF // 256, tile, 0)
        for k in range(self.value // 128):
            lanes = slice(k * 128, (k + 1) * 128)
            self.mrow[self.block(b), :] = self.wide[self.block(b), lanes]

            def token(t, carry, lanes=lanes):
                at = pl.ds(pl.multiple_of((b * BLOCK + t) * HEADS, HEADS), HEADS)
                out[at, lanes] = self.mrow[pl.ds(b * HALF + t, HEADS, stride=BLOCK), :].astype(jnp.bfloat16)
                return carry

            lax.fori_loop(0, BLOCK, token, 0, unroll=8)

    def acc(self, b, at):
        return self.s.at[2 + b, at]

    def grads(self, g):
        value, width = self.value, self.width
        for b in range(2):
            r = self.block(b)
            top, rest = self.acc(b, slice(0, value)), self.acc(b, slice(value, width))
            top[...] = dot(self.dot_t[:, r], self.p[g, r, :], NN)
            self.s[b] = dot(self.do[r, :], self.ksel[b, self.keys(g), :value], NT)
            for k in range(KEYS // 128):
                lanes = slice(k * 128, (k + 1) * 128)
                e = self.p[g, r, lanes].astype(jnp.float32)
                d = e * (self.s[b, :, lanes] * self.arow[r, :] - self.drow[r, :])
                self.p[g, r, lanes] = d.astype(jnp.bfloat16)
            dk = dot(self.qt[:, r], self.p[g, r, :], NN)
            top[...] += dk[:value]
            rest[...] = dk[value:]

    def grads_extra(self):
        value, r = self.value, self.block(1)
        self.accx[:value, :] = dot(self.dot_t[:, r], self.px[...], NN)
        dp = dot(self.do[r, :], self.kx[:, :value], NT)
        e = self.px[...].astype(jnp.float32)
        self.px[...] = (e * (dp * self.arow[r, 0:BLOCK] - self.drow[r, 0:BLOCK])).astype(jnp.bfloat16)
        dk = dot(self.qt[:, r], self.px[...], NN)
        self.accx[:value, :] += dk[:value]
        self.accx[value:, :] = dk[value:]

    def spread(self, g, m):
        lower = lax.broadcasted_iota(jnp.int32, (self.width, 128), 1) < BLOCK
        j = g * PLANE + 2 * m
        even = jnp.zeros((self.width, 128), jnp.float32)
        odd = jnp.zeros((self.width, 128), jnp.float32)
        for b in range(2):
            x = self.acc(b, slice(0, self.width))[:, m * 128:(m + 1) * 128]
            rolled = swap(x)
            w0 = self.wanted[b, j] == 1
            w1 = self.wanted[b, j + 1] == 1
            even = even + jnp.where(lower ^ w0, jnp.where(w0, rolled, x), 0.0)
            odd = odd + jnp.where(lower ^ w1, jnp.where(w1, x, rolled), 0.0)
        return even, odd

    def wide_at(self, b, n):
        at = (2 * b + n) * self.width
        return pl.ds(at, self.width)

    def grad_queries_start(self):
        for n in range(2):
            self.wide[self.wide_at(0, n), :] = jnp.zeros((self.width, HALF // 2), jnp.float32)
            rows = self.px[n * HALF // 2:(n + 1) * HALF // 2, :]
            self.wide[self.wide_at(1, n), :] = dot(self.kx[:, :self.width].T, rows, NT)

    def grad_queries(self, g):
        for b in range(2):
            kt = self.ksel[b, self.keys(g), :self.width].T
            for n in range(2):
                rows = self.p[g, b * HALF + n * HALF // 2:b * HALF + (n + 1) * HALF // 2, :]
                self.wide[self.wide_at(b, n), :] += dot(kt, rows, NT)

    def grad_queries_end(self, dq):
        lower = lax.broadcasted_iota(jnp.int32, (self.width, 128), 1) < BLOCK
        for m in range(HEADS // 2):
            n, lanes = m // 4, slice((m % 4) * 128, (m % 4 + 1) * 128)
            y0 = self.wide[self.wide_at(0, n), lanes]
            y1 = self.wide[self.wide_at(1, n), lanes]
            dq[2 * m] = jnp.where(lower, y0, swap(y1)).astype(jnp.bfloat16)
            dq[2 * m + 1] = jnp.where(lower, swap(y0), y1).astype(jnp.bfloat16)


def scratch(width, value, ranges):
    n, low, f32 = 2 * HALF, jnp.bfloat16, jnp.float32
    planes = ranges // PLANE
    return [
        pltpu.VMEM((n, width + 64), low),
        pltpu.VMEM((width, n), low),
        pltpu.VMEM((n, value), low),
        pltpu.VMEM((value, n), low),
        pltpu.VMEM((2, ranges * BLOCK, width + 64), low),
        pltpu.VMEM((BLOCK, width + 64), low),
        pltpu.VMEM((planes, HALF, KEYS), f32),
        pltpu.VMEM((planes, n, KEYS), low),
        pltpu.VMEM((HALF, BLOCK), f32),
        pltpu.VMEM((HALF, BLOCK), low),
        pltpu.VMEM((n, 128), f32),
        pltpu.VMEM((n, 128), f32),
        pltpu.VMEM((n, 128), f32),
        pltpu.VMEM((4 * width, HALF // 2), f32),
        pltpu.VMEM((width, BLOCK), f32),
    ]


def tables(chosen, shard, shards):
    tok = chosen.shape[0]
    picked = jnp.any(chosen[:, :, None] == jnp.arange(2 * shards, dtype=jnp.int32)[None, None, :], axis=1)
    grouped = picked.reshape(tok, shards, 2)
    mine = jnp.arange(shards, dtype=jnp.int32) == shard
    per_range = jnp.any(grouped, axis=2) | mine[None, :]
    first = jnp.any(chosen == 2 * shard, axis=1)
    allowed = jnp.concatenate([per_range, first[:, None], jnp.ones((tok, 31), bool)], axis=1)
    mask = jnp.where(allowed, 0.0, -BIG).astype(jnp.bfloat16)
    second = jnp.any(picked.reshape(2, BLOCK, shards, 2)[..., 1], axis=1)
    wanted = jnp.where(mine[None, :], jnp.arange(2)[:, None] == 1, second).astype(jnp.int32)
    return mask, wanted


MESH_ID = pl.DeviceIdType.MESH


def ring(v, d):
    return lax.rem(v + d + 4, 4)


class Place:
    def __init__(self):
        idx = lax.axis_index("ctx").astype(jnp.int32)
        self.idx = idx
        self.z, self.x, self.c = idx // 8, lax.rem(idx // 2, 4), lax.rem(idx, 2)
        self.y = lax.axis_index("head").astype(jnp.int32)

    def at(self, dz=0, dx=0):
        return (ring(self.z, dz) * 4 + ring(self.x, dx)) * 2 + self.c

    def near(self, axis, d):
        return {"ctx": self.at(d, 0) if axis == 0 else self.at(0, d)}

    def twin(self):
        return {"ctx": self.idx + 1 - 2 * self.c}


def greet(targets):
    barrier = pltpu.get_barrier_semaphore()
    for t in targets:
        pl.semaphore_signal(barrier, inc=1, device_id=t, device_id_type=MESH_ID)
    pl.semaphore_wait(barrier, len(targets))


class Wire:
    def __init__(self, sems):
        self.sems, self.sent = sems, []

    def send(self, src, dst, recv, target):
        copy = pltpu.make_async_remote_copy(
            src_ref=src, dst_ref=dst, send_sem=self.sems.at[len(self.sent)], recv_sem=recv,
            device_id=target, device_id_type=MESH_ID,
        )
        copy.start()
        self.sent.append(copy)

    def wait(self, dst, recv, target):
        pltpu.make_async_remote_copy(
            src_ref=dst, dst_ref=dst, send_sem=self.sems.at[0], recv_sem=recv,
            device_id=target, device_id_type=MESH_ID,
        ).wait_recv()

    def finish(self):
        for copy in self.sent:
            copy.wait_send()


class Gather:
    def __init__(self, place, wire, full, recv, twin_recv):
        self.place, self.wire, self.full, self.recv, self.twin_recv = place, wire, full, recv, twin_recv

    def source(self, h, i, j):
        return self.place.at(-i, -j) if h == 0 else self.place.at(-j, -i)

    def rows(self, h, piece=None):
        return pl.ds(h * 288, 288) if piece is None else pl.ds(h * 288 + piece * 144, 144)

    def put(self, h, i, j, second, d, piece=None):
        src = self.full.at[self.source(h, i, j), self.rows(h, piece)]
        axis = (1 - h) if second else h
        ni, nj = (i, (j + d) % 4) if second else ((i + d) % 4, j)
        sem = self.recv.at[h, ni * 4 + nj, piece or 0]
        self.wire.send(src, src, sem, self.place.near(axis, d))

    def trade(self, h, i, j):
        ref = self.full.at[self.source(h, i, j), self.rows(h)]
        self.wire.send(ref, ref, self.twin_recv.at[h, i * 4 + j], self.place.twin())

    def got(self, h, i, j):
        src = self.source(h, i, j)
        pieces = (0, 1) if (j == 2 or (j == 0 and i == 2)) else (None,)
        for piece in pieces:
            self.wire.wait(self.full.at[src, self.rows(h, piece)], self.recv.at[h, i * 4 + j, piece or 0], self.place.twin())

    def both(self, h, i, j):
        self.put(h, i, j, True, 1)
        self.put(h, i, j, True, -1)

    def start(self):
        for h in range(2):
            self.put(h, 0, 0, False, 1)
            self.put(h, 0, 0, False, -1)
        for h in range(2):
            self.both(h, 0, 0)
            self.trade(h, 0, 0)

    def first(self):
        for h in range(2):
            for i, piece, d in ((1, 0, 1), (3, 1, -1)):
                self.got(h, i, 0)
                self.put(h, i, 0, False, d, piece)
                self.both(h, i, 0)
                self.trade(h, i, 0)

    def relay(self, h, i):
        for j, piece, d in ((1, 0, 1), (3, 1, -1)):
            self.got(h, i, j)
            self.put(h, i, j, True, d, piece)
            self.trade(h, i, j)

    def second(self):
        for h in range(2):
            self.relay(h, 0)
        for h in range(2):
            self.got(h, 2, 0)
            self.both(h, 2, 0)
            self.trade(h, 2, 0)

    def third(self):
        for i in (1, 3, 2):
            for h in range(2):
                self.relay(h, i)

    def far(self, h, i):
        self.got(h, i, 2)
        self.trade(h, i, 2)

    def ready(self, k):
        for n in range(4):
            for h, i, j in ((0, k, n), (1, n, k)):
                src = self.source(h, i, j) + 1 - 2 * self.place.c
                self.wire.wait(self.full.at[src, self.rows(h)], self.twin_recv.at[h, i * 4 + j], self.place.twin())


class Ring:
    def __init__(self, place, wire, axis, block, halves, far, near, far_sem, near_sem):
        self.place, self.wire, self.axis = place, wire, axis
        self.block, self.halves = block, halves
        self.far, self.near, self.far_sem, self.near_sem = far, near, far_sem, near_sem
        me = place.z if axis == 0 else place.x
        self.to = {d: ring(me, d) for d in (0, 1, 2, -1)}

    def start(self):
        for k, d in ((0, 1), (1, -1)):
            self.wire.send(
                self.block(self.to[2]).at[self.halves[k]], self.far.at[k], self.far_sem.at[k], self.place.near(self.axis, d)
            )

    def middle(self):
        for k, d in ((0, 1), (1, -1)):
            self.wire.wait(self.far.at[k], self.far_sem.at[k], self.place.near(self.axis, -d))
            ref = self.block(self.to[d])
            part = ref[self.halves[k]].astype(jnp.float32) + self.far[k].astype(jnp.float32)
            ref[self.halves[k]] = part.astype(ref.dtype)
            self.wire.send(ref, self.near.at[k], self.near_sem.at[k], self.place.near(self.axis, d))

    def total(self):
        for k, d in ((0, 1), (1, -1)):
            self.wire.wait(self.near.at[k], self.near_sem.at[k], self.place.near(self.axis, -d))
        mine = self.block(self.to[0])[...].astype(jnp.float32)
        return mine + (self.near[0].astype(jnp.float32) + self.near[1].astype(jnp.float32))


PIECES = (pl.ds(0, 144), pl.ds(144, 144))
A_ROWS = pl.ds(0, 288)
B_ROWS = pl.ds(288, 288)


def kernel(
    wanted, mask, q_in, do_in, latent, out_hbm, dq_hbm, grad,
    q, do, full, mine, theirs, twin_in, tot_a, tot_b, head_in, head_out, result,
    far_ax, near_ax, far_az, near_az, far_bz, near_bz, far_bx, near_bx,
    local, sends, recv, twin_recv, twin_sem, sem_ax, sem_az, sem_bz, sem_bx, sem_y, *refs
):
    place = Place()
    z, x, c, y = place.z, place.x, place.c, place.y
    width = latent.shape[0]
    a = Attention(place.idx, wanted, width, do.shape[1], refs)
    out, dq = do, q
    get_q = pltpu.make_async_copy(q_in, q, local.at[0])
    get_do = pltpu.make_async_copy(do_in, do, local.at[1])
    put_out = pltpu.make_async_copy(out, out_hbm, local.at[2])
    put_dq = pltpu.make_async_copy(dq, dq_hbm, local.at[3])
    own = pltpu.make_async_copy(latent, full.at[place.idx], local.at[4])
    own.start()
    get_q.start()
    get_do.start()
    others = [{"head": ring(y, d)} for d in (1, 2, 3)]
    greet([place.near(0, 1), place.near(0, -1), place.near(1, 1), place.near(1, -1), place.twin()] + others)
    own.wait()
    wire = Wire(sends)

    def each(count, step):
        def body(g, carry):
            step(g)
            return carry

        lax.fori_loop(0, count, body, 0)

    g = Gather(place, wire, full, recv, twin_recv)
    g.start()
    get_q.wait()
    a.load_queries(q, mask)
    g.first()
    get_do.wait()
    a.load_cotangent(do)
    g.second()
    g.far(0, 0)
    g.ready(0)
    a.pick(full, z)
    a.pick_own(full[place.idx])
    a.scores(z, 0, True)
    g.third()
    g.far(0, 1)
    g.far(0, 3)
    for k in (1, 3):
        g.ready(k)

    def follow(k):
        plane = ring(z, -k)

        @pl.when(plane < z)
        def _():
            a.pick(full, plane)
            a.scores(plane, 0, False)

    g.far(0, 2)
    for i in (0, 1, 3, 2):
        g.far(1, i)
    follow(1)
    follow(3)
    g.ready(2)
    follow(2)
    for b in range(2):
        if b == 1:
            a.scores(z, b, True)
            each(z, lambda g: a.scores(g, 1, False))
        a.softmax_start(b)
        each(z + 1, lambda g, b=b: a.softmax(g, b))
        a.softmax_end(b, out)
    put_out.start()
    a.grads_extra()

    order = [ring(z, 2), ring(z, 1), ring(z, -1), z]

    def make(g, last):
        @pl.when(g <= z)
        def _():
            a.grads(g)
            for m in range(4):
                even, odd = a.spread(g, m)
                mine[g, m] = jnp.where(c == 0, even, odd).astype(mine.dtype)
                theirs[g, m] = jnp.where(c == 0, odd, even).astype(mine.dtype)

        if last:
            mine[g, x, :, :BLOCK] = (mine[g, x, :, :BLOCK].astype(jnp.float32) + a.accx[...]).astype(mine.dtype)
        else:
            @pl.when(g > z)
            def _():
                for m in range(4):
                    mine[g, m] = jnp.zeros(mine.shape[2:], mine.dtype)
                    theirs[g, m] = jnp.zeros(mine.shape[2:], mine.dtype)

        wire.send(theirs.at[g], twin_in.at[g], twin_sem.at[g], place.twin())

    def join(g):
        wire.wait(twin_in.at[g], twin_sem.at[g], place.twin())
        for m in range(4):
            mine[g, m] = (mine[g, m].astype(jnp.float32) + twin_in[g, m].astype(jnp.float32)).astype(mine.dtype)

    a_rings = [
        Ring(
            place, wire, 1, lambda t, g=g: mine.at[g, t, A_ROWS], PIECES,
            far_ax.at[g], near_ax.at[g], sem_ax.at[g, 0], sem_ax.at[g, 1],
        )
        for g in order
    ]
    b_ring = Ring(
        place, wire, 0, lambda t: mine.at[t, :, B_ROWS], (pl.ds(0, 2), pl.ds(2, 2)), far_bz, near_bz, sem_bz.at[0], sem_bz.at[1]
    )
    a_last = Ring(place, wire, 0, lambda t: tot_a.at[t], PIECES, far_az, near_az, sem_az.at[0], sem_az.at[1])
    b_last = Ring(place, wire, 1, lambda t: tot_b.at[t], PIECES, far_bx, near_bx, sem_bx.at[0], sem_bx.at[1])

    def settle(n):
        tot_a[order[n]] = a_rings[n].total().astype(tot_a.dtype)

    make(order[0], False)
    make(order[1], False)
    join(order[0])
    b_ring.start()
    a_rings[0].start()
    make(order[2], False)
    join(order[1])
    a_rings[1].start()
    a_rings[0].middle()
    make(order[3], True)
    join(order[2])
    b_ring.middle()
    a_rings[2].start()
    a_rings[1].middle()
    settle(0)
    a_last.start()
    put_out.wait()
    a.grad_queries_start()

    def queries(n):
        if n == 3:
            a.grad_queries(order[n])
            return

        @pl.when(order[n] < z)
        def _():
            a.grad_queries(order[n])

    join(order[3])
    a_rings[3].start()
    a_rings[2].middle()
    settle(1)
    queries(0)
    tot_b[...] = b_ring.total().astype(tot_b.dtype)
    b_last.start()
    a_rings[3].middle()
    settle(2)
    a_last.middle()
    queries(1)
    settle(3)
    b_last.middle()
    queries(2)
    low = a_last.total().astype(jnp.bfloat16)
    high = b_last.total().astype(jnp.bfloat16)
    for n in range(2):
        head_out[n] = low[n * 144:(n + 1) * 144]
        head_out[n + 2] = high[n * 144:(n + 1) * 144]
    for d in (1, 2, 3):
        wire.send(head_out.at[ring(y, d)], head_in.at[d - 1], sem_y.at[0, d - 1], others[d - 1])
    queries(3)
    for d in (1, 2, 3):
        wire.wait(head_in.at[d - 1], sem_y.at[0, d - 1], others[d - 1])
    total = head_out[y].astype(jnp.float32) + head_in[0].astype(jnp.float32)
    total = total + (head_in[1].astype(jnp.float32) + head_in[2].astype(jnp.float32))
    result[y] = total.astype(jnp.bfloat16)
    for d in (1, 2, 3):
        wire.send(result.at[y], result.at[y], sem_y.at[1, d - 1], others[d - 1])
    a.grad_queries_end(dq)
    put_dq.start()
    for d in (1, 2, 3):
        wire.wait(result.at[ring(y, -d)], sem_y.at[1, d - 1], others[d - 1])
    for n in range(4):
        grad[n * 144:(n + 1) * 144, :] = result[n].astype(jnp.float32)
    put_dq.wait()
    wire.finish()


def body(queries, latent, cotangent, selection):
    tok, heads, width = queries.shape
    value = cotangent.shape[2]
    shards = lax.axis_size("ctx")
    shard = lax.axis_index("ctx").astype(jnp.int32)
    mask, wanted = tables(selection, shard, shards)
    vmem = pl.BlockSpec(memory_space=pltpu.VMEM)
    smem = pl.BlockSpec(memory_space=pltpu.SMEM)
    hbm = pl.BlockSpec(memory_space=pl.ANY)
    dma = pltpu.SemaphoreType.DMA
    low = jnp.bfloat16
    half, piece = width // 2, width // 4
    out, dq, grad = pl.pallas_call(
        kernel,
        out_shape=(
            jax.ShapeDtypeStruct((heads * tok, value), low),
            jax.ShapeDtypeStruct((heads, width, tok), low),
            jax.ShapeDtypeStruct((width, tok), jnp.float32),
        ),
        in_specs=[smem, vmem, hbm, hbm, vmem],
        out_specs=(hbm, hbm, vmem),
        scratch_shapes=[
            pltpu.VMEM((heads, width, tok), low),
            pltpu.VMEM((heads * tok, value), low),
            pltpu.VMEM((shards, width, tok), low),
            pltpu.VMEM((4, 4, width, tok), low),
            pltpu.VMEM((4, 4, width, tok), low),
            pltpu.VMEM((4, 4, width, tok), low),
            pltpu.VMEM((4, half, tok), low),
            pltpu.VMEM((4, half, tok), low),
            pltpu.VMEM((3, piece, tok), low),
            pltpu.VMEM((4, piece, tok), low),
            pltpu.VMEM((4, piece, tok), low),
            pltpu.VMEM((4, 2, piece, tok), low),
            pltpu.VMEM((4, 2, half, tok), low),
            pltpu.VMEM((2, piece, tok), low),
            pltpu.VMEM((2, half, tok), low),
            pltpu.VMEM((2, 2, half, tok), low),
            pltpu.VMEM((2, 4, half, tok), low),
            pltpu.VMEM((2, piece, tok), low),
            pltpu.VMEM((2, half, tok), low),
            dma((5,)), dma((112,)), dma((2, 16, 2)), dma((2, 16)),
            dma((4,)), dma((4, 2, 2)), dma((2, 2)), dma((2, 2)), dma((2, 2)), dma((2, 3)),
        ] + scratch(width, value, shards),
        compiler_params=pltpu.CompilerParams(collective_id=0, has_side_effects=True, vmem_limit_bytes=67043328),
    )(wanted, mask, queries.transpose(1, 2, 0), cotangent.reshape(tok * heads, value), latent.T)
    return out.reshape(tok, heads, value), dq.transpose(2, 0, 1), grad.T


def solution(mesh):
    placed = (P("ctx", "head", None), P("ctx", None), P("ctx", "head", None), P("ctx", None))
    return jax.shard_map(
        body,
        mesh=mesh,
        in_specs=placed,
        out_specs=(P("ctx", "head", None), P("ctx", "head", None), P("ctx", None)),
        check_vma=False,
    )
```

```python
import functools

import jax
import jax.numpy as jnp
from jax import lax
from jax.experimental import pallas as pl
from jax.experimental.pallas import tpu as pltpu
from jax.sharding import PartitionSpec as P

BLOCK = 64
SCALE = 192.0 ** (-0.5)
LOG2E = 1.4426950408889634
BIG = 1e30
PLANE = 8
KEYS = PLANE * BLOCK
HEADS = 16
HALF = HEADS * BLOCK
NT = (((1,), (1,)), ((), ()))
NN = (((1,), (0,)), ((), ()))


def dot(a, b, dims):
    return lax.dot_general(a, b, dims, preferred_element_type=jnp.float32)


def swap(x):
    return pltpu.roll(x, 64, 1)


class Attention:
    def __init__(self, shard, wanted, width, value, refs):
        self.shard, self.wanted, self.width, self.value = shard, wanted, width, value
        (self.qx, self.qt, self.do, self.dot_t, self.ksel, self.kx, self.s, self.p, self.sx, self.px,
         self.mrow, self.arow, self.drow, self.wide, self.accx) = refs
        self.pad = self.qx.shape[1] - width

    def keys(self, g):
        return pl.ds(pl.multiple_of(g * KEYS, KEYS), KEYS)

    def block(self, b):
        return slice(b * HALF, (b + 1) * HALF)

    def load_queries(self, q, mask):
        width = self.width
        lower = lax.broadcasted_iota(jnp.int32, (width, 128), 1) < BLOCK

        def pair(m, carry):
            q0 = q[2 * m].astype(jnp.float32)
            q1 = q[2 * m + 1].astype(jnp.float32)
            for b in range(2):
                x = jnp.where(lower, q0, swap(q1)) if b == 0 else jnp.where(lower, swap(q0), q1)
                x = x.astype(jnp.bfloat16)
                at = pl.ds(pl.multiple_of(b * HALF + m * 128, 128), 128)
                self.qt[:, at] = x
                self.qx[at, :width] = x.T
                bias = mask[b * BLOCK:(b + 1) * BLOCK, :].astype(jnp.bfloat16)
                self.qx[at, width:] = jnp.concatenate([bias, bias], axis=0)
            return carry

        lax.fori_loop(0, HEADS // 2, pair, 0)

    def load_cotangent(self, do):
        for b in range(2):
            for pair in range(self.value // 256):
                for k in range(2):
                    lanes = slice((2 * pair + k) * 128, (2 * pair + k + 1) * 128)
                    self.mrow[self.block(k), :] = do[self.block(b), lanes].astype(jnp.float32)

                def head(h, carry, b=b, pair=pair):
                    at = pl.ds(pl.multiple_of(b * HALF + h * BLOCK, BLOCK), BLOCK)
                    for k in range(2):
                        rows = self.mrow[pl.ds(k * HALF + h, BLOCK, stride=HEADS), :]
                        lanes = slice((2 * pair + k) * 128, (2 * pair + k + 1) * 128)
                        self.do[at, lanes] = rows.astype(jnp.bfloat16)
                    return carry

                lax.fori_loop(0, HEADS, head, 0)

    def pick(self, latent, g):
        width = self.width
        lower = lax.broadcasted_iota(jnp.int32, (width, 128), 1) < BLOCK
        column = lax.broadcasted_iota(jnp.int32, (128, self.pad), 1)
        slot = lax.broadcasted_iota(jnp.int32, (128, self.pad), 0) // BLOCK

        def pair(m, carry):
            j = g * PLANE + 2 * m
            k0 = latent[j].astype(jnp.float32)
            k1 = latent[j + 1].astype(jnp.float32)
            r0, r1 = swap(k0), swap(k1)
            at = pl.ds(pl.multiple_of(j * BLOCK, 128), 128)
            for b in range(2):
                w0, w1 = self.wanted[b, j] == 1, self.wanted[b, j + 1] == 1
                x = jnp.where(lower, jnp.where(w0, r0, k0), jnp.where(w1, k1, r1)).astype(jnp.bfloat16)
                self.ksel[b, at, :width] = x.T
                self.ksel[b, at, width:] = jnp.where(column == j + slot, 1.0, 0.0).astype(jnp.bfloat16)
            return carry

        lax.fori_loop(0, PLANE // 2, pair, 0)

    def pick_own(self, own):
        self.kx[:, :self.width] = own.T[:BLOCK, :]
        column = lax.broadcasted_iota(jnp.int32, (BLOCK, self.pad), 1)
        self.kx[:, self.width:] = jnp.where(column == 32, 1.0, 0.0).astype(jnp.bfloat16)

    def scores(self, g, b, own):
        r = self.block(b)
        x = dot(self.qx[r, :], self.ksel[b, self.keys(g), :], NT)
        if own:
            lane = lax.broadcasted_iota(jnp.int32, (HALF, KEYS), 1)
            row = lax.broadcasted_iota(jnp.int32, (HALF, KEYS), 0)
            late = (lane // BLOCK == lax.rem(self.shard, PLANE)) & (lane % BLOCK > row % BLOCK)
            x = jnp.where(late, -BIG, x)
        self.s[g] = x
        top = jnp.maximum(self.s[g, :, 0:128], self.s[g, :, 128:256])
        for k in range(2, KEYS // 128):
            top = jnp.maximum(top, self.s[g, :, k * 128:(k + 1) * 128])
        if own:
            if b == 1:
                y = dot(self.qx[r, :], self.kx[...], NT)
                self.sx[...] = y
                top = jnp.maximum(top, jnp.concatenate([y, y], axis=1))
            self.mrow[r, :] = top
        else:
            self.mrow[r, :] = jnp.maximum(self.mrow[r, :], top)

    def softmax_start(self, b):
        c = SCALE * LOG2E
        r = self.block(b)
        top = jnp.max(self.mrow[r, :], axis=1, keepdims=True) * c
        self.mrow[r, :] = jnp.broadcast_to(top, (HALF, 128))
        if b == 0:
            self.wide[r, :] = jnp.zeros((HALF, self.value), jnp.float32)
            self.arow[r, :] = jnp.zeros((HALF, 128), jnp.float32)
        else:
            e = jnp.exp2(self.sx[...] * c - top)
            self.arow[r, :] = jnp.concatenate([e, jnp.zeros_like(e)], axis=1)
            self.px[...] = e.astype(jnp.bfloat16)
            self.wide[r, :] = dot(self.px[...], self.kx[:, :self.value], NN)

    def softmax(self, g, b):
        c = SCALE * LOG2E
        r = self.block(b)
        total = self.arow[r, :]
        for k in range(KEYS // 128):
            lanes = slice(k * 128, (k + 1) * 128)
            e = jnp.exp2(self.s[g, :, lanes] * c - self.mrow[r, :])
            total = total + e
            self.p[g, r, lanes] = e.astype(jnp.bfloat16)
        self.arow[r, :] = total
        self.wide[r, :] += dot(self.p[g, r, :], self.ksel[b, self.keys(g), :self.value], NN)

    def softmax_end(self, b, out):
        def tile(t, carry):
            r = pl.ds(pl.multiple_of(b * HALF + t * 256, 256), 256)
            inv = 1.0 / jnp.sum(self.arow[r, :], axis=1, keepdims=True)
            low = (self.wide[r, :] * inv).astype(jnp.bfloat16)
            out[r, :] = low
            do = self.do[r, :].astype(jnp.float32)
            delta = jnp.sum(do * low.astype(jnp.float32), axis=1, keepdims=True)
            self.dot_t[:, r] = (do * inv).astype(jnp.bfloat16).T
            self.arow[r, :] = jnp.broadcast_to(inv * SCALE, (256, 128))
            self.drow[r, :] = jnp.broadcast_to(inv * SCALE * delta, (256, 128))
            return carry

        lax.fori_loop(0, HALF // 256, tile, 0)
    def acc(self, b, at):
        return self.s.at[2 + b, at]

    def grads(self, g, b):
        value, width = self.value, self.width
        r = self.block(b)
        top, rest = self.acc(b, slice(0, value)), self.acc(b, slice(value, width))
        top[...] = dot(self.dot_t[:, r], self.p[g, r, :], NN)
        self.s[b] = dot(self.do[r, :], self.ksel[b, self.keys(g), :value], NT)
        for k in range(KEYS // 128):
            lanes = slice(k * 128, (k + 1) * 128)
            e = self.p[g, r, lanes].astype(jnp.float32)
            d = e * (self.s[b, :, lanes] * self.arow[r, :] - self.drow[r, :])
            self.p[g, r, lanes] = d.astype(jnp.bfloat16)
        dk = dot(self.qt[:, r], self.p[g, r, :], NN)
        top[...] += dk[:value]
        rest[...] = dk[value:]

    def grads_extra(self):
        value, r = self.value, self.block(1)
        self.accx[:value, :] = dot(self.dot_t[:, r], self.px[...], NN)
        dp = dot(self.do[r, :], self.kx[:, :value], NT)
        e = self.px[...].astype(jnp.float32)
        self.px[...] = (e * (dp * self.arow[r, 0:BLOCK] - self.drow[r, 0:BLOCK])).astype(jnp.bfloat16)
        dk = dot(self.qt[:, r], self.px[...], NN)
        self.accx[:value, :] += dk[:value]
        self.accx[value:, :] = dk[value:]

    def spread(self, g, m):
        lower = lax.broadcasted_iota(jnp.int32, (self.width, 128), 1) < BLOCK
        j = g * PLANE + 2 * m
        even = jnp.zeros((self.width, 128), jnp.float32)
        odd = jnp.zeros((self.width, 128), jnp.float32)
        for b in range(2):
            x = self.acc(b, slice(0, self.width))[:, m * 128:(m + 1) * 128]
            rolled = swap(x)
            w0 = self.wanted[b, j] == 1
            w1 = self.wanted[b, j + 1] == 1
            even = even + jnp.where(lower ^ w0, jnp.where(w0, rolled, x), 0.0)
            odd = odd + jnp.where(lower ^ w1, jnp.where(w1, x, rolled), 0.0)
        return even, odd

    def wide_at(self, b, n):
        at = (2 * b + n) * self.width
        return pl.ds(at, self.width)

    def grad_queries_start(self):
        for n in range(2):
            self.wide[self.wide_at(0, n), :] = jnp.zeros((self.width, HALF // 2), jnp.float32)
            rows = self.px[n * HALF // 2:(n + 1) * HALF // 2, :]
            self.wide[self.wide_at(1, n), :] = dot(self.kx[:, :self.width].T, rows, NT)

    def grad_queries(self, g):
        for b in range(2):
            kt = self.ksel[b, self.keys(g), :self.width].T
            for n in range(2):
                rows = self.p[g, b * HALF + n * HALF // 2:b * HALF + (n + 1) * HALF // 2, :]
                self.wide[self.wide_at(b, n), :] += dot(kt, rows, NT)

    def grad_queries_end(self, dq):
        lower = lax.broadcasted_iota(jnp.int32, (self.width, 128), 1) < BLOCK
        for m in range(HEADS // 2):
            n, lanes = m // 4, slice((m % 4) * 128, (m % 4 + 1) * 128)
            y0 = self.wide[self.wide_at(0, n), lanes]
            y1 = self.wide[self.wide_at(1, n), lanes]
            dq[2 * m] = jnp.where(lower, y0, swap(y1)).astype(jnp.bfloat16)
            dq[2 * m + 1] = jnp.where(lower, swap(y0), y1).astype(jnp.bfloat16)


def scratch(width, value, ranges):
    n, low, f32 = 2 * HALF, jnp.bfloat16, jnp.float32
    planes = ranges // PLANE
    return [
        pltpu.VMEM((n, width + 64), low),
        pltpu.VMEM((width, n), low),
        pltpu.VMEM((n, value), low),
        pltpu.VMEM((value, n), low),
        pltpu.VMEM((2, ranges * BLOCK, width + 64), low),
        pltpu.VMEM((BLOCK, width + 64), low),
        pltpu.VMEM((planes, HALF, KEYS), f32),
        pltpu.VMEM((planes, n, KEYS), low),
        pltpu.VMEM((HALF, BLOCK), f32),
        pltpu.VMEM((HALF, BLOCK), low),
        pltpu.VMEM((n, 128), f32),
        pltpu.VMEM((n, 128), f32),
        pltpu.VMEM((n, 128), f32),
        pltpu.VMEM((4 * width, HALF // 2), f32),
        pltpu.VMEM((width, BLOCK), f32),
    ]


def tables(chosen, shard, shards):
    tok, picks = chosen.shape
    column = jnp.arange(64, dtype=jnp.int32)[None, None, :]
    listed = chosen[:, :, None]
    hit = (listed >> 1 == column) | (column == shards) & (listed == 2 * shard) | (column > shards)
    mask = jnp.max(jnp.where(hit, 0.0, -BIG), axis=1)
    half = chosen.reshape(2, tok // 2, picks, 1)
    ranges = jnp.arange(shards, dtype=jnp.int32)[None, None, None, :]
    second = jnp.arange(2, dtype=jnp.int32)[:, None, None, None] == 1
    hit = jnp.where(ranges == shard, second, half == 2 * ranges + 1)
    wanted = jnp.max(jnp.where(hit, 1, 0), axis=(1, 2))
    return mask, wanted


MESH_ID = pl.DeviceIdType.MESH


def ring(v, d):
    return lax.rem(v + d + 4, 4)


class Place:
    def __init__(self):
        idx = lax.axis_index("ctx").astype(jnp.int32)
        self.idx = idx
        self.z, self.x, self.c = idx // 8, lax.rem(idx // 2, 4), lax.rem(idx, 2)
        self.y = lax.axis_index("head").astype(jnp.int32)

    def at(self, dz=0, dx=0):
        return (ring(self.z, dz) * 4 + ring(self.x, dx)) * 2 + self.c

    def near(self, axis, d):
        return {"ctx": self.at(d, 0) if axis == 0 else self.at(0, d)}

    def twin(self):
        return {"ctx": self.idx + 1 - 2 * self.c}


def greet(targets):
    barrier = pltpu.get_barrier_semaphore()
    for t in targets:
        pl.semaphore_signal(barrier, inc=1, device_id=t, device_id_type=MESH_ID)
    pl.semaphore_wait(barrier, len(targets))


class Wire:
    def __init__(self, sems):
        self.sems, self.sent, self.done = sems, [], 0

    def send(self, src, dst, recv, target):
        copy = pltpu.make_async_remote_copy(
            src_ref=src, dst_ref=dst, send_sem=self.sems.at[len(self.sent)], recv_sem=recv,
            device_id=target, device_id_type=MESH_ID,
        )
        copy.start()
        self.sent.append(copy)

    def wait(self, dst, recv, target):
        pltpu.make_async_remote_copy(
            src_ref=dst, dst_ref=dst, send_sem=self.sems.at[0], recv_sem=recv,
            device_id=target, device_id_type=MESH_ID,
        ).wait_recv()

    def finish(self):
        for copy in self.sent[self.done:]:
            copy.wait_send()
        self.done = len(self.sent)


class Gather:
    def __init__(self, place, wire, full, recv, twin_recv):
        self.place, self.wire, self.full, self.recv, self.twin_recv = place, wire, full, recv, twin_recv

    def source(self, h, i, j):
        return self.place.at(-i, -j) if h == 0 else self.place.at(-j, -i)

    def rows(self, h, piece=None):
        return pl.ds(h * 288, 288) if piece is None else pl.ds(h * 288 + piece * 144, 144)

    def put(self, h, i, j, second, d, piece=None):
        src = self.full.at[self.source(h, i, j), self.rows(h, piece)]
        axis = (1 - h) if second else h
        ni, nj = (i, (j + d) % 4) if second else ((i + d) % 4, j)
        sem = self.recv.at[h, ni * 4 + nj, piece or 0]
        self.wire.send(src, src, sem, self.place.near(axis, d))

    def trade(self, h, i, j):
        ref = self.full.at[self.source(h, i, j), self.rows(h)]
        self.wire.send(ref, ref, self.twin_recv.at[h, i * 4 + j], self.place.twin())

    def got(self, h, i, j):
        src = self.source(h, i, j)
        pieces = (0, 1) if (j == 2 or (j == 0 and i == 2)) else (None,)
        for piece in pieces:
            self.wire.wait(self.full.at[src, self.rows(h, piece)], self.recv.at[h, i * 4 + j, piece or 0], self.place.twin())

    def both(self, h, i, j):
        self.put(h, i, j, True, 1)
        self.put(h, i, j, True, -1)

    def start(self):
        for h in range(2):
            self.put(h, 0, 0, False, 1)
            self.put(h, 0, 0, False, -1)
        for h in range(2):
            self.both(h, 0, 0)
            self.trade(h, 0, 0)

    def first(self):
        for h in range(2):
            for i, piece, d in ((1, 0, 1), (3, 1, -1)):
                self.got(h, i, 0)
                self.put(h, i, 0, False, d, piece)
                self.both(h, i, 0)
                self.trade(h, i, 0)

    def relay(self, h, i):
        for j, piece, d in ((1, 0, 1), (3, 1, -1)):
            self.got(h, i, j)
            self.put(h, i, j, True, d, piece)
            self.trade(h, i, j)

    def second(self):
        for h in range(2):
            self.relay(h, 0)
        for h in range(2):
            self.got(h, 2, 0)
            self.both(h, 2, 0)
            self.trade(h, 2, 0)

    def third(self):
        for i in (1, 3, 2):
            for h in range(2):
                self.relay(h, i)

    def far(self, h, i):
        self.got(h, i, 2)
        self.trade(h, i, 2)

    def ready(self, k):
        for n in range(4):
            for h, i, j in ((0, k, n), (1, n, k)):
                src = self.source(h, i, j) + 1 - 2 * self.place.c
                self.wire.wait(self.full.at[src, self.rows(h)], self.twin_recv.at[h, i * 4 + j], self.place.twin())


class Ring:
    def __init__(self, place, wire, axis, block, halves, far, near, far_sem, near_sem):
        self.place, self.wire, self.axis = place, wire, axis
        self.block, self.halves = block, halves
        self.far, self.near, self.far_sem, self.near_sem = far, near, far_sem, near_sem
        me = place.z if axis == 0 else place.x
        self.to = {d: ring(me, d) for d in (0, 1, 2, -1)}

    def start(self):
        for k, d in ((0, 1), (1, -1)):
            self.wire.send(
                self.block(self.to[2]).at[self.halves[k]], self.far.at[k], self.far_sem.at[k], self.place.near(self.axis, d)
            )

    def middle(self, ways=(0, 1)):
        for k in ways:
            d = 1 - 2 * k
            self.wire.wait(self.far.at[k], self.far_sem.at[k], self.place.near(self.axis, -d))
            ref = self.block(self.to[d])
            part = ref[self.halves[k]].astype(jnp.float32) + self.far[k].astype(jnp.float32)
            ref[self.halves[k]] = part.astype(ref.dtype)
            self.wire.send(ref, self.near.at[k], self.near_sem.at[k], self.place.near(self.axis, d))

    def total(self):
        for k, d in ((0, 1), (1, -1)):
            self.wire.wait(self.near.at[k], self.near_sem.at[k], self.place.near(self.axis, -d))
        mine = self.block(self.to[0])[...].astype(jnp.float32)
        return mine + (self.near[0].astype(jnp.float32) + self.near[1].astype(jnp.float32))


PIECES = (pl.ds(0, 144), pl.ds(144, 144))
A_ROWS = pl.ds(0, 288)
B_ROWS = pl.ds(288, 288)


def kernel(
    wanted, mask, q_in, do_in, latent, out_hbm, dq_hbm, grad,
    q, do, full, mine, twin_in, tot_a, tot_b, head_in, head_out, result,
    far_ax, near_ax, far_az, near_az, far_bz, near_bz, far_bx, near_bx,
    local, sends, recv, twin_recv, twin_sem, sem_ax, sem_az, sem_bz, sem_bx, sem_y, *refs
):
    place = Place()
    z, x, c, y = place.z, place.x, place.c, place.y
    width = latent.shape[0]
    a = Attention(place.idx, wanted, width, do.shape[1], refs)
    out, dq = do, q
    get_q = pltpu.make_async_copy(q_in, q, local.at[0])
    get_do = pltpu.make_async_copy(do_in, do, local.at[1])
    put_out = pltpu.make_async_copy(out, out_hbm, local.at[2])
    put_dq = pltpu.make_async_copy(dq, dq_hbm, local.at[3])
    own = pltpu.make_async_copy(latent, full.at[place.idx], local.at[4])
    own.start()
    get_q.start()
    get_do.start()
    others = [{"head": ring(y, d)} for d in (1, 2, 3)]
    greet([place.near(0, 1), place.near(0, -1), place.near(1, 1), place.near(1, -1), place.twin()] + others)
    own.wait()
    wire = Wire(sends)

    def each(count, step):
        def body(g, carry):
            step(g)
            return carry

        lax.fori_loop(0, count, body, 0)

    g = Gather(place, wire, full, recv, twin_recv)
    g.start()
    get_q.wait()
    a.load_queries(q, mask)
    g.first()
    get_do.wait()
    a.load_cotangent(do)
    g.second()
    g.far(0, 0)
    g.ready(0)
    a.pick(full, z)
    a.pick_own(full[place.idx])
    a.scores(z, 0, True)
    g.third()
    g.far(0, 1)
    g.far(0, 3)
    for k in (1, 3):
        g.ready(k)

    def follow(k):
        plane = ring(z, -k)

        @pl.when(plane < z)
        def _():
            a.pick(full, plane)
            a.scores(plane, 0, False)

    g.far(0, 2)
    for i in (0, 1, 3, 2):
        g.far(1, i)
    follow(1)
    follow(3)
    g.ready(2)
    follow(2)
    for b in range(2):
        if b == 1:
            a.scores(z, b, True)
            each(z, lambda g: a.scores(g, 1, False))
        a.softmax_start(b)
        each(z + 1, lambda g, b=b: a.softmax(g, b))
        a.softmax_end(b, out)
    put_out.start()
    a.grads_extra()
    wire.finish()

    order = [ring(z, 2), ring(z, 1), ring(z, -1), z]

    def make(g, last, meanwhile):
        @pl.when(g <= z)
        def _():
            a.grads(g, 0)

        meanwhile()

        @pl.when(g <= z)
        def _():
            a.grads(g, 1)
            for m in range(4):
                even, odd = a.spread(g, m)
                mine[g, m] = jnp.where(c == 0, even, odd).astype(mine.dtype)
                full[4 * g + m] = jnp.where(c == 0, odd, even).astype(mine.dtype)

        if last:
            mine[g, x, :, :BLOCK] = (mine[g, x, :, :BLOCK].astype(jnp.float32) + a.accx[...]).astype(mine.dtype)
        else:
            @pl.when(g > z)
            def _():
                for m in range(4):
                    mine[g, m] = jnp.zeros(mine.shape[2:], mine.dtype)
                    full[4 * g + m] = jnp.zeros(mine.shape[2:], mine.dtype)

        wire.send(full.at[pl.ds(4 * g, 4)], twin_in.at[g], twin_sem.at[g], place.twin())

    def join(g):
        wire.wait(twin_in.at[g], twin_sem.at[g], place.twin())
        for m in range(4):
            mine[g, m] = (mine[g, m].astype(jnp.float32) + twin_in[g, m].astype(jnp.float32)).astype(mine.dtype)

    a_rings = [
        Ring(
            place, wire, 1, lambda t, g=g: mine.at[g, t, A_ROWS], PIECES,
            far_ax.at[g], near_ax.at[g], sem_ax.at[g, 0], sem_ax.at[g, 1],
        )
        for g in order
    ]
    b_ring = Ring(
        place, wire, 0, lambda t: mine.at[t, :, B_ROWS], (pl.ds(0, 2), pl.ds(2, 2)), far_bz, near_bz, sem_bz.at[0], sem_bz.at[1]
    )
    a_last = Ring(place, wire, 0, lambda t: tot_a.at[t], PIECES, far_az, near_az, sem_az.at[0], sem_az.at[1])
    b_last = Ring(place, wire, 1, lambda t: tot_b.at[t], PIECES, far_bx, near_bx, sem_bx.at[0], sem_bx.at[1])

    def settle(n):
        tot_a[order[n]] = a_rings[n].total().astype(tot_a.dtype)

    def queries(n):
        if n == 3:
            a.grad_queries(order[n])
            return

        @pl.when(order[n] < z)
        def _():
            a.grad_queries(order[n])

    def during_1():
        join(order[0])
        b_ring.start()
        a_rings[0].start()

    def during_2():
        join(order[1])
        b_ring.middle((0,))
        a_rings[1].start()
        a_rings[0].middle()

    def during_3():
        join(order[2])
        b_ring.middle((1,))
        a_rings[2].start()
        a_rings[1].middle()
        settle(0)
        a_last.start()

    make(order[0], False, lambda: None)
    make(order[1], False, during_1)
    make(order[2], False, during_2)
    make(order[3], True, during_3)
    a_rings[2].middle()
    settle(1)
    put_out.wait()
    a.grad_queries_start()
    queries(0)
    join(order[3])
    a_rings[3].start()
    tot_b[...] = b_ring.total().astype(tot_b.dtype)
    b_last.start()
    settle(2)
    a_last.middle()
    queries(1)
    a_rings[3].middle()
    b_last.middle()
    queries(2)
    settle(3)
    low = a_last.total().astype(jnp.bfloat16)
    high = b_last.total().astype(jnp.bfloat16)
    for n in range(2):
        head_out[n] = low[n * 144:(n + 1) * 144]
        head_out[n + 2] = high[n * 144:(n + 1) * 144]
    for d in (1, 2, 3):
        wire.send(head_out.at[ring(y, d)], head_in.at[d - 1], sem_y.at[0, d - 1], others[d - 1])
    queries(3)
    for d in (1, 2, 3):
        wire.wait(head_in.at[d - 1], sem_y.at[0, d - 1], others[d - 1])
    total = head_out[y].astype(jnp.float32) + head_in[0].astype(jnp.float32)
    total = total + (head_in[1].astype(jnp.float32) + head_in[2].astype(jnp.float32))
    result[y] = total.astype(jnp.bfloat16)
    for d in (1, 2, 3):
        wire.send(result.at[y], result.at[y], sem_y.at[1, d - 1], others[d - 1])
    a.grad_queries_end(dq)
    put_dq.start()
    for d in (1, 2, 3):
        wire.wait(result.at[ring(y, -d)], sem_y.at[1, d - 1], others[d - 1])
    for n in range(4):
        grad[n * 144:(n + 1) * 144, :] = result[n].astype(jnp.float32)
    put_dq.wait()
    wire.finish()


def body(queries, latent, cotangent, selection):
    tok, heads, width = queries.shape
    value = cotangent.shape[2]
    shards = lax.axis_size("ctx")
    shard = lax.axis_index("ctx").astype(jnp.int32)
    mask, wanted = tables(selection, shard, shards)
    vmem = pl.BlockSpec(memory_space=pltpu.VMEM)
    smem = pl.BlockSpec(memory_space=pltpu.SMEM)
    hbm = pl.BlockSpec(memory_space=pl.ANY)
    dma = pltpu.SemaphoreType.DMA
    low = jnp.bfloat16
    half, piece = width // 2, width // 4
    out, dq, grad = pl.pallas_call(
        kernel,
        out_shape=(
            jax.ShapeDtypeStruct((heads * tok, value), low),
            jax.ShapeDtypeStruct((heads, width, tok), low),
            jax.ShapeDtypeStruct((width, tok), jnp.float32),
        ),
        in_specs=[smem, vmem, hbm, hbm, vmem],
        out_specs=(hbm, hbm, vmem),
        scratch_shapes=[
            pltpu.VMEM((heads, width, tok), low),
            pltpu.VMEM((heads * tok, value), low),
            pltpu.VMEM((shards, width, tok), low),
            pltpu.VMEM((4, 4, width, tok), low),
            pltpu.VMEM((4, 4, width, tok), low),
            pltpu.VMEM((4, half, tok), low),
            pltpu.VMEM((4, half, tok), low),
            pltpu.VMEM((3, piece, tok), low),
            pltpu.VMEM((4, piece, tok), low),
            pltpu.VMEM((4, piece, tok), low),
            pltpu.VMEM((4, 2, piece, tok), low),
            pltpu.VMEM((4, 2, half, tok), low),
            pltpu.VMEM((2, piece, tok), low),
            pltpu.VMEM((2, half, tok), low),
            pltpu.VMEM((2, 2, half, tok), low),
            pltpu.VMEM((2, 4, half, tok), low),
            pltpu.VMEM((2, piece, tok), low),
            pltpu.VMEM((2, half, tok), low),
            dma((5,)), dma((112,)), dma((2, 16, 2)), dma((2, 16)),
            dma((4,)), dma((4, 2, 2)), dma((2, 2)), dma((2, 2)), dma((2, 2)), dma((2, 3)),
        ] + scratch(width, value, shards),
        compiler_params=pltpu.CompilerParams(collective_id=0, has_side_effects=True, vmem_limit_bytes=67043328),
    )(wanted, mask, queries.transpose(1, 2, 0), cotangent.reshape(tok * heads, value), latent.T)
    out = out.reshape(2, heads, BLOCK, value).transpose(0, 2, 1, 3)
    return out.reshape(tok, heads, value), dq.transpose(2, 0, 1), grad.T


def solution(mesh):
    placed = (P("ctx", "head", None), P("ctx", None), P("ctx", "head", None), P("ctx", None))
    return jax.shard_map(
        body,
        mesh=mesh,
        in_specs=placed,
        out_specs=(P("ctx", "head", None), P("ctx", "head", None), P("ctx", None)),
        check_vma=False,
    )
```

```python
import functools

import jax
import jax.numpy as jnp
import numpy as np
from jax import lax
from jax.experimental import pallas as pl
from jax.experimental.pallas import tpu as pltpu
from jax.sharding import PartitionSpec as P

BLOCK = 64
SCALE = 192.0 ** (-0.5)
LOG2E = 1.4426950408889634
BIG = 1e30
PLANE = 8
KEYS = PLANE * BLOCK
HEADS = 16
HALF = HEADS * BLOCK
NT = (((1,), (1,)), ((), ()))
NN = (((1,), (0,)), ((), ()))


def dot(a, b, dims):
    return lax.dot_general(a, b, dims, preferred_element_type=jnp.float32)


def swap(x):
    return pltpu.roll(x, 64, 1)


class Attention:
    def __init__(self, shard, wanted, width, value, refs):
        self.shard, self.wanted, self.width, self.value = shard, wanted, width, value
        (self.qx, self.qt, self.do, self.dot_t, self.ksel, self.kx, self.s, self.p, self.sx, self.px,
         self.mrow, self.arow, self.drow, self.wide, self.accx) = refs
        self.pad = self.qx.shape[1] - width
        self.shards = self.ksel.shape[1] // BLOCK

    def keys(self, g):
        return pl.ds(pl.multiple_of(g * KEYS, KEYS), KEYS)

    def block(self, b):
        return slice(b * HALF, (b + 1) * HALF)

    def second(self, b, j):
        return jnp.where(j == self.shard, b, self.wanted[b * self.shards + j]) == 1

    def load_mask(self, chosen, mask):
        column = lax.broadcasted_iota(jnp.int32, mask.shape, 1)
        bias = jnp.where(column > self.shards, 0.0, -BIG)
        lists = chosen[...].T
        for n in range(lists.shape[1]):
            listed = lists[:, n:n + 1]
            hit = (listed >> 1 == column) | ((column == self.shards) & (listed == 2 * self.shard))
            bias = jnp.where(hit, 0.0, bias)
        mask[...] = bias.astype(mask.dtype)

    def load_queries(self, q, mask):
        width = self.width
        lower = lax.broadcasted_iota(jnp.int32, (width, 128), 1) < BLOCK

        def pair(m, carry):
            q0 = q[2 * m].astype(jnp.float32)
            q1 = q[2 * m + 1].astype(jnp.float32)
            for b in range(2):
                x = jnp.where(lower, q0, swap(q1)) if b == 0 else jnp.where(lower, swap(q0), q1)
                x = x.astype(jnp.bfloat16)
                at = pl.ds(pl.multiple_of(b * HALF + m * 128, 128), 128)
                self.qt[:, at] = x
                self.qx[at, :width] = x.T
                bias = mask[b * BLOCK:(b + 1) * BLOCK, :]
                self.qx[at, width:] = jnp.concatenate([bias, bias], axis=0)
            return carry

        lax.fori_loop(0, HEADS // 2, pair, 0)

    def load_cotangent(self, do):
        for b in range(2):
            for pair in range(self.value // 256):
                for k in range(2):
                    lanes = slice((2 * pair + k) * 128, (2 * pair + k + 1) * 128)
                    self.mrow[self.block(k), :] = do[self.block(b), lanes].astype(jnp.float32)

                def head(h, carry, b=b, pair=pair):
                    at = pl.ds(pl.multiple_of(b * HALF + h * BLOCK, BLOCK), BLOCK)
                    for k in range(2):
                        rows = self.mrow[pl.ds(k * HALF + h, BLOCK, stride=HEADS), :]
                        lanes = slice((2 * pair + k) * 128, (2 * pair + k + 1) * 128)
                        self.do[at, lanes] = rows.astype(jnp.bfloat16)
                    return carry

                lax.fori_loop(0, HEADS, head, 0)

    def pick(self, latent, g):
        width = self.width
        lower = lax.broadcasted_iota(jnp.int32, (width, 128), 1) < BLOCK
        column = lax.broadcasted_iota(jnp.int32, (128, self.pad), 1)
        slot = lax.broadcasted_iota(jnp.int32, (128, self.pad), 0) // BLOCK

        def pair(m, carry):
            j = g * PLANE + 2 * m
            k0 = latent[j].astype(jnp.float32)
            k1 = latent[j + 1].astype(jnp.float32)
            r0, r1 = swap(k0), swap(k1)
            at = pl.ds(pl.multiple_of(j * BLOCK, 128), 128)
            for b in range(2):
                w0, w1 = self.second(b, j), self.second(b, j + 1)
                x = jnp.where(lower, jnp.where(w0, r0, k0), jnp.where(w1, k1, r1)).astype(jnp.bfloat16)
                self.ksel[b, at, :width] = x.T
                self.ksel[b, at, width:] = jnp.where(column == j + slot, 1.0, 0.0).astype(jnp.bfloat16)
            return carry

        lax.fori_loop(0, PLANE // 2, pair, 0)

    def pick_own(self, own):
        self.kx[:, :self.width] = own.T[:BLOCK, :]
        column = lax.broadcasted_iota(jnp.int32, (BLOCK, self.pad), 1)
        self.kx[:, self.width:] = jnp.where(column == 32, 1.0, 0.0).astype(jnp.bfloat16)

    def scores(self, g, b, own):
        r = self.block(b)
        x = dot(self.qx[r, :], self.ksel[b, self.keys(g), :], NT)
        if own:
            lane = lax.broadcasted_iota(jnp.int32, (HALF, KEYS), 1)
            row = lax.broadcasted_iota(jnp.int32, (HALF, KEYS), 0)
            late = (lane // BLOCK == lax.rem(self.shard, PLANE)) & (lane % BLOCK > row % BLOCK)
            x = jnp.where(late, -BIG, x)
        self.s[g] = x
        top = jnp.maximum(self.s[g, :, 0:128], self.s[g, :, 128:256])
        for k in range(2, KEYS // 128):
            top = jnp.maximum(top, self.s[g, :, k * 128:(k + 1) * 128])
        if own:
            if b == 1:
                y = dot(self.qx[r, :], self.kx[...], NT)
                self.sx[...] = y
                top = jnp.maximum(top, jnp.concatenate([y, y], axis=1))
            self.mrow[r, :] = top
        else:
            self.mrow[r, :] = jnp.maximum(self.mrow[r, :], top)

    def softmax_start(self, b):
        c = SCALE * LOG2E
        r = self.block(b)
        top = jnp.max(self.mrow[r, :], axis=1, keepdims=True) * c
        self.mrow[r, :] = jnp.broadcast_to(top, (HALF, 128))
        if b == 0:
            self.wide[r, :] = jnp.zeros((HALF, self.value), jnp.float32)
            self.arow[r, :] = jnp.zeros((HALF, 128), jnp.float32)
        else:
            e = jnp.exp2(self.sx[...] * c - top)
            self.arow[r, :] = jnp.concatenate([e, jnp.zeros_like(e)], axis=1)
            self.px[...] = e.astype(jnp.bfloat16)
            self.wide[r, :] = dot(self.px[...], self.kx[:, :self.value], NN)

    def softmax(self, g, b):
        c = SCALE * LOG2E
        r = self.block(b)
        total = self.arow[r, :]
        for k in range(KEYS // 128):
            lanes = slice(k * 128, (k + 1) * 128)
            e = jnp.exp2(self.s[g, :, lanes] * c - self.mrow[r, :])
            total = total + e
            self.p[g, r, lanes] = e.astype(jnp.bfloat16)
        self.arow[r, :] = total
        self.wide[r, :] += dot(self.p[g, r, :], self.ksel[b, self.keys(g), :self.value], NN)

    def softmax_end(self, b, out):
        def tile(t, carry):
            r = pl.ds(pl.multiple_of(b * HALF + t * 256, 256), 256)
            inv = 1.0 / jnp.sum(self.arow[r, :], axis=1, keepdims=True)
            low = (self.wide[r, :] * inv).astype(jnp.bfloat16)
            out[r, :] = low
            do = self.do[r, :].astype(jnp.float32)
            delta = jnp.sum(do * low.astype(jnp.float32), axis=1, keepdims=True)
            self.dot_t[:, r] = (do * inv).astype(jnp.bfloat16).T
            self.arow[r, :] = jnp.broadcast_to(inv * SCALE, (256, 128))
            self.drow[r, :] = jnp.broadcast_to(inv * SCALE * delta, (256, 128))
            return carry

        lax.fori_loop(0, HALF // 256, tile, 0)
    def acc(self, b, at):
        return self.s.at[2 + b, at]

    def grads(self, g, b):
        value, width = self.value, self.width
        r = self.block(b)
        top, rest = self.acc(b, slice(0, value)), self.acc(b, slice(value, width))
        top[...] = dot(self.dot_t[:, r], self.p[g, r, :], NN)
        self.s[b] = dot(self.do[r, :], self.ksel[b, self.keys(g), :value], NT)
        for k in range(KEYS // 128):
            lanes = slice(k * 128, (k + 1) * 128)
            e = self.p[g, r, lanes].astype(jnp.float32)
            d = e * (self.s[b, :, lanes] * self.arow[r, :] - self.drow[r, :])
            self.p[g, r, lanes] = d.astype(jnp.bfloat16)
        dk = dot(self.qt[:, r], self.p[g, r, :], NN)
        top[...] += dk[:value]
        rest[...] = dk[value:]

    def grads_extra(self):
        value, r = self.value, self.block(1)
        self.accx[:value, :] = dot(self.dot_t[:, r], self.px[...], NN)
        dp = dot(self.do[r, :], self.kx[:, :value], NT)
        e = self.px[...].astype(jnp.float32)
        self.px[...] = (e * (dp * self.arow[r, 0:BLOCK] - self.drow[r, 0:BLOCK])).astype(jnp.bfloat16)
        dk = dot(self.qt[:, r], self.px[...], NN)
        self.accx[:value, :] += dk[:value]
        self.accx[value:, :] = dk[value:]

    def spread(self, g, m):
        lower = lax.broadcasted_iota(jnp.int32, (self.width, 128), 1) < BLOCK
        j = g * PLANE + 2 * m
        even = jnp.zeros((self.width, 128), jnp.float32)
        odd = jnp.zeros((self.width, 128), jnp.float32)
        for b in range(2):
            x = self.acc(b, slice(0, self.width))[:, m * 128:(m + 1) * 128]
            rolled = swap(x)
            w0 = self.second(b, j)
            w1 = self.second(b, j + 1)
            even = even + jnp.where(lower ^ w0, jnp.where(w0, rolled, x), 0.0)
            odd = odd + jnp.where(lower ^ w1, jnp.where(w1, x, rolled), 0.0)
        return even, odd

    def wide_at(self, b, n):
        at = (2 * b + n) * self.width
        return pl.ds(at, self.width)

    def grad_queries_start(self):
        for n in range(2):
            self.wide[self.wide_at(0, n), :] = jnp.zeros((self.width, HALF // 2), jnp.float32)
            rows = self.px[n * HALF // 2:(n + 1) * HALF // 2, :]
            self.wide[self.wide_at(1, n), :] = dot(self.kx[:, :self.width].T, rows, NT)

    def grad_queries(self, g):
        for b in range(2):
            kt = self.ksel[b, self.keys(g), :self.width].T
            for n in range(2):
                rows = self.p[g, b * HALF + n * HALF // 2:b * HALF + (n + 1) * HALF // 2, :]
                self.wide[self.wide_at(b, n), :] += dot(kt, rows, NT)

    def grad_queries_end(self, dq):
        lower = lax.broadcasted_iota(jnp.int32, (self.width, 128), 1) < BLOCK
        for m in range(HEADS // 2):
            n, lanes = m // 4, slice((m % 4) * 128, (m % 4 + 1) * 128)
            y0 = self.wide[self.wide_at(0, n), lanes]
            y1 = self.wide[self.wide_at(1, n), lanes]
            dq[2 * m] = jnp.where(lower, y0, swap(y1)).astype(jnp.bfloat16)
            dq[2 * m + 1] = jnp.where(lower, swap(y0), y1).astype(jnp.bfloat16)


def scratch(width, value, ranges):
    n, low, f32 = 2 * HALF, jnp.bfloat16, jnp.float32
    planes = ranges // PLANE
    return [
        pltpu.VMEM((n, width + 64), low),
        pltpu.VMEM((width, n), low),
        pltpu.VMEM((n, value), low),
        pltpu.VMEM((value, n), low),
        pltpu.VMEM((2, ranges * BLOCK, width + 64), low),
        pltpu.VMEM((BLOCK, width + 64), low),
        pltpu.VMEM((planes, HALF, KEYS), f32),
        pltpu.VMEM((planes, n, KEYS), low),
        pltpu.VMEM((HALF, BLOCK), f32),
        pltpu.VMEM((HALF, BLOCK), low),
        pltpu.VMEM((n, 128), f32),
        pltpu.VMEM((n, 128), f32),
        pltpu.VMEM((n, 128), f32),
        pltpu.VMEM((4 * width, HALF // 2), f32),
        pltpu.VMEM((width, BLOCK), f32),
    ]


def choices(chosen, shards):
    token = np.arange(chosen.shape[0], dtype=np.int32)
    entry = np.arange(2 * shards, dtype=np.int32)
    mark = chosen + jnp.asarray(token // BLOCK * 128)[:, None]
    wanted = jnp.asarray(2 * (entry % shards) + 1 + entry // shards * 128)
    return jnp.max((mark[:, :, None] == wanted[None, None, :]).astype(jnp.int32), axis=(0, 1))


MESH_ID = pl.DeviceIdType.MESH


def ring(v, d):
    return lax.rem(v + d + 4, 4)


class Place:
    def __init__(self):
        idx = lax.axis_index("ctx").astype(jnp.int32)
        self.idx = idx
        self.z, self.x, self.c = idx // 8, lax.rem(idx // 2, 4), lax.rem(idx, 2)
        self.y = lax.axis_index("head").astype(jnp.int32)

    def at(self, dz=0, dx=0):
        return (ring(self.z, dz) * 4 + ring(self.x, dx)) * 2 + self.c

    def near(self, axis, d):
        return {"ctx": self.at(d, 0) if axis == 0 else self.at(0, d)}

    def twin(self):
        return {"ctx": self.idx + 1 - 2 * self.c}


def greet(targets):
    barrier = pltpu.get_barrier_semaphore()
    for t in targets:
        pl.semaphore_signal(barrier, inc=1, device_id=t, device_id_type=MESH_ID)
    pl.semaphore_wait(barrier, len(targets))


class Wire:
    def __init__(self, sems):
        self.sems, self.sent, self.done = sems, [], 0

    def send(self, src, dst, recv, target):
        copy = pltpu.make_async_remote_copy(
            src_ref=src, dst_ref=dst, send_sem=self.sems.at[len(self.sent)], recv_sem=recv,
            device_id=target, device_id_type=MESH_ID,
        )
        copy.start()
        self.sent.append(copy)

    def wait(self, dst, recv, target):
        pltpu.make_async_remote_copy(
            src_ref=dst, dst_ref=dst, send_sem=self.sems.at[0], recv_sem=recv,
            device_id=target, device_id_type=MESH_ID,
        ).wait_recv()

    def finish(self):
        for copy in self.sent[self.done:]:
            copy.wait_send()
        self.done = len(self.sent)


class Gather:
    def __init__(self, place, wire, full, recv, twin_recv):
        self.place, self.wire, self.full, self.recv, self.twin_recv = place, wire, full, recv, twin_recv

    def source(self, h, i, j):
        return self.place.at(-i, -j) if h == 0 else self.place.at(-j, -i)

    def rows(self, h, piece=None):
        return pl.ds(h * 288, 288) if piece is None else pl.ds(h * 288 + piece * 144, 144)

    def put(self, h, i, j, second, d, piece=None):
        src = self.full.at[self.source(h, i, j), self.rows(h, piece)]
        axis = (1 - h) if second else h
        ni, nj = (i, (j + d) % 4) if second else ((i + d) % 4, j)
        sem = self.recv.at[h, ni * 4 + nj, piece or 0]
        self.wire.send(src, src, sem, self.place.near(axis, d))

    def trade(self, h, i, j):
        ref = self.full.at[self.source(h, i, j), self.rows(h)]
        self.wire.send(ref, ref, self.twin_recv.at[h, i * 4 + j], self.place.twin())

    def got(self, h, i, j):
        src = self.source(h, i, j)
        pieces = (0, 1) if (j == 2 or (j == 0 and i == 2)) else (None,)
        for piece in pieces:
            self.wire.wait(self.full.at[src, self.rows(h, piece)], self.recv.at[h, i * 4 + j, piece or 0], self.place.twin())

    def both(self, h, i, j):
        self.put(h, i, j, True, 1)
        self.put(h, i, j, True, -1)

    def start(self):
        for h in range(2):
            self.put(h, 0, 0, False, 1)
            self.put(h, 0, 0, False, -1)
        for h in range(2):
            self.both(h, 0, 0)
            self.trade(h, 0, 0)

    def first(self):
        for h in range(2):
            for i, piece, d in ((1, 0, 1), (3, 1, -1)):
                self.got(h, i, 0)
                self.put(h, i, 0, False, d, piece)
                self.both(h, i, 0)
                self.trade(h, i, 0)

    def relay(self, h, i):
        for j, piece, d in ((1, 0, 1), (3, 1, -1)):
            self.got(h, i, j)
            self.put(h, i, j, True, d, piece)
            self.trade(h, i, j)

    def second(self):
        for h in range(2):
            self.relay(h, 0)
        for h in range(2):
            self.got(h, 2, 0)
            self.both(h, 2, 0)
            self.trade(h, 2, 0)

    def third(self):
        for i in (1, 3, 2):
            for h in range(2):
                self.relay(h, i)

    def far(self, h, i):
        self.got(h, i, 2)
        self.trade(h, i, 2)

    def ready(self, k):
        for n in range(4):
            for h, i, j in ((0, k, n), (1, n, k)):
                src = self.source(h, i, j) + 1 - 2 * self.place.c
                self.wire.wait(self.full.at[src, self.rows(h)], self.twin_recv.at[h, i * 4 + j], self.place.twin())


class Ring:
    def __init__(self, place, wire, axis, block, halves, far, near, far_sem, near_sem):
        self.place, self.wire, self.axis = place, wire, axis
        self.block, self.halves = block, halves
        self.far, self.near, self.far_sem, self.near_sem = far, near, far_sem, near_sem
        me = place.z if axis == 0 else place.x
        self.to = {d: ring(me, d) for d in (0, 1, 2, -1)}

    def start(self):
        for k, d in ((0, 1), (1, -1)):
            self.wire.send(
                self.block(self.to[2]).at[self.halves[k]], self.far.at[k], self.far_sem.at[k], self.place.near(self.axis, d)
            )

    def middle(self, ways=(0, 1)):
        for k in ways:
            d = 1 - 2 * k
            self.wire.wait(self.far.at[k], self.far_sem.at[k], self.place.near(self.axis, -d))
            ref = self.block(self.to[d])
            part = ref[self.halves[k]].astype(jnp.float32) + self.far[k].astype(jnp.float32)
            ref[self.halves[k]] = part.astype(ref.dtype)
            self.wire.send(ref, self.near.at[k], self.near_sem.at[k], self.place.near(self.axis, d))

    def total(self):
        for k, d in ((0, 1), (1, -1)):
            self.wire.wait(self.near.at[k], self.near_sem.at[k], self.place.near(self.axis, -d))
        mine = self.block(self.to[0])[...].astype(jnp.float32)
        return mine + (self.near[0].astype(jnp.float32) + self.near[1].astype(jnp.float32))


A, B = 384, 192
A_ROWS, B_ROWS = pl.ds(0, A), pl.ds(A, B)
A_PIECES = (pl.ds(0, A // 2), pl.ds(A // 2, A // 2))
B_PIECES = (pl.ds(0, B // 2), pl.ds(B // 2, B // 2))


def kernel(
    wanted, chosen, q_in, do_in, latent, out_hbm, dq_hbm, grad,
    mask, q, do, full, mine, twin_in, tot_a, tot_b, head_in, head_out, result,
    far_ax, near_ax, far_az, near_az, far_bz, near_bz, far_bx, near_bx,
    local, sends, recv, twin_recv, twin_sem, sem_ax, sem_az, sem_bz, sem_bx, sem_y, *refs
):
    place = Place()
    z, x, c, y = place.z, place.x, place.c, place.y
    width = latent.shape[0]
    a = Attention(place.idx, wanted, width, do.shape[1], refs)
    out, dq = do, q
    get_q = pltpu.make_async_copy(q_in, q, local.at[0])
    get_do = pltpu.make_async_copy(do_in, do, local.at[1])
    put_out = pltpu.make_async_copy(out, out_hbm, local.at[2])
    put_dq = pltpu.make_async_copy(dq, dq_hbm, local.at[3])
    own = pltpu.make_async_copy(latent, full.at[place.idx], local.at[4])
    own.start()
    get_q.start()
    get_do.start()
    others = [{"head": ring(y, d)} for d in (1, 2, 3)]
    greet([place.near(0, 1), place.near(0, -1), place.near(1, 1), place.near(1, -1), place.twin()] + others)
    own.wait()
    wire = Wire(sends)

    def each(count, step):
        def body(g, carry):
            step(g)
            return carry

        lax.fori_loop(0, count, body, 0)

    g = Gather(place, wire, full, recv, twin_recv)
    g.start()
    a.load_mask(chosen, mask)
    get_q.wait()
    a.load_queries(q, mask)
    g.first()
    get_do.wait()
    a.load_cotangent(do)
    g.second()
    g.far(0, 0)
    g.ready(0)
    a.pick(full, z)
    a.pick_own(full[place.idx])
    a.scores(z, 0, True)
    g.third()
    g.far(0, 1)
    g.far(0, 3)
    for k in (1, 3):
        g.ready(k)

    def follow(k):
        plane = ring(z, -k)

        @pl.when(plane < z)
        def _():
            a.pick(full, plane)
            a.scores(plane, 0, False)

    g.far(0, 2)
    for i in (0, 1, 3, 2):
        g.far(1, i)
    each(2, lambda n: follow(2 * n + 1))
    g.ready(2)
    follow(2)
    for b in range(2):
        if b == 1:
            a.scores(z, b, True)
            each(z, lambda g: a.scores(g, 1, False))
        a.softmax_start(b)
        each(z + 1, lambda g, b=b: a.softmax(g, b))
        a.softmax_end(b, out)
    put_out.start()
    a.grads_extra()
    wire.finish()

    order = [ring(z, 2), ring(z, 1), ring(z, -1), z]

    def make(g, last, meanwhile):
        @pl.when(g <= z)
        def _():
            a.grads(g, 0)

        meanwhile()

        @pl.when(g <= z)
        def _():
            a.grads(g, 1)
            for m in range(4):
                even, odd = a.spread(g, m)
                mine[g, m] = jnp.where(c == 0, even, odd).astype(mine.dtype)
                full[4 * g + m] = jnp.where(c == 0, odd, even).astype(mine.dtype)

        if last:
            mine[g, x, :, :BLOCK] = (mine[g, x, :, :BLOCK].astype(jnp.float32) + a.accx[...]).astype(mine.dtype)
        else:
            @pl.when(g > z)
            def _():
                for m in range(4):
                    mine[g, m] = jnp.zeros(mine.shape[2:], mine.dtype)
                    full[4 * g + m] = jnp.zeros(mine.shape[2:], mine.dtype)

        wire.send(full.at[pl.ds(4 * g, 4)], twin_in.at[g], twin_sem.at[g], place.twin())

    def join(g):
        wire.wait(twin_in.at[g], twin_sem.at[g], place.twin())
        for m in range(4):
            mine[g, m] = (mine[g, m].astype(jnp.float32) + twin_in[g, m].astype(jnp.float32)).astype(mine.dtype)

    a_rings = [
        Ring(
            place, wire, 1, lambda t, g=g: mine.at[g, t, A_ROWS], A_PIECES,
            far_ax.at[g], near_ax.at[g], sem_ax.at[g, 0], sem_ax.at[g, 1],
        )
        for g in order
    ]
    b_ring = Ring(
        place, wire, 0, lambda t: mine.at[t, :, B_ROWS], (pl.ds(0, 2), pl.ds(2, 2)), far_bz, near_bz, sem_bz.at[0], sem_bz.at[1]
    )
    a_last = Ring(place, wire, 0, lambda t: tot_a.at[t], A_PIECES, far_az, near_az, sem_az.at[0], sem_az.at[1])
    b_last = Ring(place, wire, 1, lambda t: tot_b.at[t], B_PIECES, far_bx, near_bx, sem_bx.at[0], sem_bx.at[1])

    def settle(n):
        tot_a[order[n]] = a_rings[n].total().astype(tot_a.dtype)

    def queries(n):
        if n == 3:
            a.grad_queries(order[n])
            return

        @pl.when(order[n] < z)
        def _():
            a.grad_queries(order[n])

    def during_1():
        join(order[0])
        b_ring.start()
        a_rings[0].start()

    def during_2():
        join(order[1])
        b_ring.middle((0,))
        a_rings[1].start()
        a_rings[0].middle()

    def during_3():
        join(order[2])
        b_ring.middle((1,))
        a_rings[2].start()
        a_rings[1].middle()
        settle(0)
        a_last.start()

    make(order[0], False, lambda: None)
    make(order[1], False, during_1)
    make(order[2], False, during_2)
    make(order[3], True, during_3)
    a_rings[2].middle()
    settle(1)
    put_out.wait()
    a.grad_queries_start()
    queries(0)
    join(order[3])
    a_rings[3].start()
    tot_b[...] = b_ring.total().astype(tot_b.dtype)
    b_last.start()
    settle(2)
    a_last.middle()
    queries(1)
    a_rings[3].middle()
    b_last.middle()
    queries(2)
    settle(3)
    low = a_last.total().astype(jnp.bfloat16)
    high = b_last.total().astype(jnp.bfloat16)
    both = jnp.concatenate([low, high], axis=0)
    for n in range(4):
        head_out[n] = both[n * 144:(n + 1) * 144]
    for d in (1, 2, 3):
        wire.send(head_out.at[ring(y, d)], head_in.at[d - 1], sem_y.at[0, d - 1], others[d - 1])
    queries(3)
    for d in (1, 2, 3):
        wire.wait(head_in.at[d - 1], sem_y.at[0, d - 1], others[d - 1])
    total = head_out[y].astype(jnp.float32) + head_in[0].astype(jnp.float32)
    total = total + (head_in[1].astype(jnp.float32) + head_in[2].astype(jnp.float32))
    result[y] = total.astype(jnp.bfloat16)
    for d in (1, 2, 3):
        wire.send(result.at[y], result.at[y], sem_y.at[1, d - 1], others[d - 1])
    a.grad_queries_end(dq)
    put_dq.start()
    for d in (1, 2, 3):
        wire.wait(result.at[ring(y, -d)], sem_y.at[1, d - 1], others[d - 1])
    for n in range(4):
        grad[n * 144:(n + 1) * 144, :] = result[n].astype(jnp.float32)
    put_dq.wait()
    wire.finish()


def body(queries, latent, cotangent, selection):
    tok, heads, width = queries.shape
    value = cotangent.shape[2]
    shards = lax.axis_size("ctx")
    wanted = choices(selection, shards)
    vmem = pl.BlockSpec(memory_space=pltpu.VMEM)
    smem = pl.BlockSpec(memory_space=pltpu.SMEM)
    hbm = pl.BlockSpec(memory_space=pl.ANY)
    dma = pltpu.SemaphoreType.DMA
    low = jnp.bfloat16
    piece = width // 4
    out, dq, grad = pl.pallas_call(
        kernel,
        out_shape=(
            jax.ShapeDtypeStruct((heads * tok, value), low),
            jax.ShapeDtypeStruct((heads, width, tok), low),
            jax.ShapeDtypeStruct((width, tok), jnp.float32),
        ),
        in_specs=[smem, vmem, hbm, hbm, vmem],
        out_specs=(hbm, hbm, vmem),
        scratch_shapes=[
            pltpu.VMEM((tok, 64), low),
            pltpu.VMEM((heads, width, tok), low),
            pltpu.VMEM((heads * tok, value), low),
            pltpu.VMEM((shards, width, tok), low),
            pltpu.VMEM((4, 4, width, tok), low),
            pltpu.VMEM((4, 4, width, tok), low),
            pltpu.VMEM((4, A, tok), low),
            pltpu.VMEM((4, B, tok), low),
            pltpu.VMEM((3, piece, tok), low),
            pltpu.VMEM((4, piece, tok), low),
            pltpu.VMEM((4, piece, tok), low),
            pltpu.VMEM((4, 2, A // 2, tok), low),
            pltpu.VMEM((4, 2, A, tok), low),
            pltpu.VMEM((2, A // 2, tok), low),
            pltpu.VMEM((2, A, tok), low),
            pltpu.VMEM((2, 2, B, tok), low),
            pltpu.VMEM((2, 4, B, tok), low),
            pltpu.VMEM((2, B // 2, tok), low),
            pltpu.VMEM((2, B, tok), low),
            dma((5,)), dma((112,)), dma((2, 16, 2)), dma((2, 16)),
            dma((4,)), dma((4, 2, 2)), dma((2, 2)), dma((2, 2)), dma((2, 2)), dma((2, 3)),
        ] + scratch(width, value, shards),
        compiler_params=pltpu.CompilerParams(collective_id=0, has_side_effects=True, vmem_limit_bytes=67043328),
    )(wanted, selection.T, queries.transpose(1, 2, 0), cotangent.reshape(tok * heads, value), latent.T)
    out = out.reshape(2, heads, BLOCK, value).transpose(0, 2, 1, 3)
    return out.reshape(tok, heads, value), dq.transpose(2, 0, 1), grad.T


def solution(mesh):
    placed = (P("ctx", "head", None), P("ctx", None), P("ctx", "head", None), P("ctx", None))
    return jax.shard_map(
        body,
        mesh=mesh,
        in_specs=placed,
        out_specs=(P("ctx", "head", None), P("ctx", "head", None), P("ctx", None)),
        check_vma=False,
    )
```
